32 devices in a mesh: grp: 2 (over y), vec: 4 (over z), wlk: 4 (over x, core).
Axes of the slice: x: 2, y: 2, z: 4, core: 2. Of those that a mesh axis runs over, the one named last changes fastest.
Arguments:
- cholesky: bfloat16 [48, 64, 512], P(('grp', 'vec')), parts along dimension 0
- orbitals: float32 [32, 64, 512], P(('grp', 'vec', 'wlk')), parts along dimension 0, may hold values from -6 to 6
- log_weights: float32 [32], P(('grp', 'vec', 'wlk')), parts along dimension 0, may hold values from -6 to 6
- parents: int32 [32], P(('grp', 'vec', 'wlk')), parts along dimension 0, may hold values from 0 to 3
- propagator: float32 [1024, 512], P('grp'), parts along dimension 0
Outputs:
- new_orbitals: float32 [32, 64, 512], P(('grp', 'vec', 'wlk')), parts along dimension 0
- new_log_weights: float32 [32], P(('grp', 'vec', 'wlk')), parts along dimension 0
The draws below stay inside these ranges and needn't reach their ends.
There are 2 independent parts, one for each index of `grp`. The reference program is written for one: setup_inputs(seed, part) draws one part's arguments, and reference() takes and returns one part's arrays. A program takes and returns all parts, laid end to end along the dimension named above; each array names one. Nothing has to cross between parts.
Inputs may be any that keep to these rules, and one draw needn't show every extreme that they name: parents[w] counts within the aligned block of 4 consecutive walkers that holds w.
All inputs are finite; a program needn't handle non-finite values.
Results may differ from the reference program's by a relative error of at most 0.02.
Values may be sent and summed in bfloat16 or wider, within the bound.
A program may use at most 64 MiB of HBM per device.

```python
import math
import jax
import jax.numpy as jnp
import numpy as np
from jax import lax

NORB = 512
NOCC = 64
NS_ITERS = 2
NCHOL = 24
POPULATION = 4
WALKERS = 16


def draw_cholesky(key, part):
    noise_key = jax.random.fold_in(key, 11)
    position = jnp.arange(NCHOL, dtype=jnp.float32) / max(NCHOL - 1, 1)
    samples = jax.random.normal(noise_key, (NCHOL, NOCC, NORB), jnp.float32)
    falloff = 3.0 ** (1.0 - position)
    return (samples * falloff[:, None, None] / math.sqrt(NORB)).astype(jnp.bfloat16)


def draw_orbitals(key, part):
    noise_key = jax.random.fold_in(key, 37)
    values = jnp.clip(jax.random.normal(noise_key, (WALKERS, NOCC, NORB), jnp.float32), -6.0, 6.0)
    return values.astype(jnp.float32)


def draw_propagator(key, part):
    noise_key = jax.random.fold_in(key, 23)
    samples = jax.random.normal(noise_key, (NORB, NORB), jnp.float32)
    return jnp.eye(NORB, dtype=jnp.float32) + 0.5 * samples / math.sqrt(NORB)


def set_ends(result, stream_key, least, top_value):
    place = [jax.random.randint(jax.random.fold_in(stream_key, axis), (), 0, length) for axis, length in enumerate(result.shape)]
    main_axis = result.shape.index(max(result.shape))
    beside = place[:main_axis] + [(place[main_axis] + 1) % result.shape[main_axis]] + place[main_axis + 1:]
    return result.at[tuple(place)].set(least).at[tuple(beside)].set(top_value)


def block_scale(own_key, extent, shards, smallest, top_value):
    level = 1.0
    for dim, parts in shards:
        steps = jax.random.uniform(jax.random.fold_in(jax.random.fold_in(own_key, 6), dim), (parts,), jnp.float32, smallest / len(shards), top_value / len(shards))
        level = level * jnp.repeat(jnp.exp(steps), extent[dim] // parts).reshape((-1,) + (1,) * (len(extent) - 1 - dim))
    return level


def cumulative_ranks(count, lean):
    weights = [(1 << 20) // math.isqrt(standing ** lean) + 1 for standing in range(1, count + 1)]
    deviation = 1 + sum(weights) // (1 << 30)
    return np.cumsum(np.array([max(1, weight // deviation) for weight in weights]))


def ranked(key, shape, number_of, slope):
    table = cumulative_ranks(number_of, slope)
    ticket = jax.random.randint(jax.random.fold_in(key, 1), shape, 0, int(table[number_of - 1]))
    rank = jnp.searchsorted(jnp.asarray(table, jnp.int32), ticket, side="right")
    return jax.random.permutation(jax.random.fold_in(key, 2), number_of)[rank].astype(jnp.int32)


def gaussian(stream_key, dims, scale, limit, cuts=(), held_as=jnp.bfloat16):
    loudness = block_scale(stream_key, dims, cuts, -0.22, 0.18) if cuts else 1.0
    result = jax.random.normal(stream_key, dims, jnp.float32) * scale * loudness
    return jnp.minimum(jnp.maximum(result, -limit), limit).astype(held_as)


def setup_inputs(seed: int = 0, part: int = 0) -> dict:
    key_list = jax.random.split(jax.random.key(seed), 6)
    part_splits = jax.random.split(jax.random.fold_in(key_list[5], part), 6)
    return {
        "cholesky": draw_cholesky(jax.random.fold_in(jax.random.fold_in(key_list[5], part), 71), part),
        "orbitals": draw_orbitals(jax.random.fold_in(jax.random.fold_in(key_list[5], part), 71), part),
        "log_weights": gaussian(part_splits[2], (WALKERS,), 1.0, 6.0, ((0, 16),), jnp.float32),
        "parents": set_ends(ranked(part_splits[3], (WALKERS,), POPULATION, 2), jax.random.fold_in(part_splits[3], 3), 0, POPULATION - 1).astype(jnp.int32),
        "propagator": draw_propagator(jax.random.fold_in(jax.random.fold_in(key_list[5], part), 71), part),
    }


gradient_step = 0.25
energy_step = 0.002
epsilon = 1e-06

def reference(cholesky, orbitals, log_weights, parents, propagator):
    norm_scale = 1.0 / math.sqrt(NCHOL)
    chol_flat = cholesky.astype(jnp.float32).reshape(NCHOL * NOCC, NORB)
    identity = jnp.eye(NOCC, dtype=jnp.float32)

    def per_walker(orbital_rows):
        rounded = orbital_rows.astype(jnp.bfloat16)
        rounded = lax.optimization_barrier(rounded)
        theta = rounded.astype(jnp.float32)
        product = jnp.dot(theta, chol_flat.T)
        product = lax.optimization_barrier(product.astype(jnp.bfloat16))
        blocks = product.astype(jnp.float32).reshape(NOCC, NCHOL, NOCC)
        traces = lax.optimization_barrier(jnp.sum(blocks * identity[:, None, :], axis=(0, 2)))
        swapped = jnp.transpose(blocks, (2, 1, 0))
        exchange_sum = lax.optimization_barrier(jnp.sum(blocks * swapped, axis=(0, 2)))
        energy = 0.5 * norm_scale * jnp.sum(traces * traces - exchange_sum)
        adjoint = norm_scale * (traces[None, :, None] * identity[:, None, :] - swapped)
        adjoint = lax.optimization_barrier(adjoint.astype(jnp.bfloat16))
        adjoint = adjoint.astype(jnp.float32).reshape(NOCC, NCHOL * NOCC)
        gradient = jnp.dot(adjoint, chol_flat)
        return (energy, gradient)
    energies, gradients = lax.map(per_walker, orbitals)
    stepped = orbitals - gradient_step * gradients
    shifted = log_weights - energy_step * energies
    walker_ids = jnp.arange(WALKERS, dtype=jnp.int32)
    source = walker_ids // POPULATION * POPULATION + parents.astype(jnp.int32)
    chosen = stepped[source]
    new_log_weights = shifted[source]
    propagated = jnp.einsum('wjq,pq->wjp', chosen, propagator, precision=lax.Precision.HIGHEST)
    mean_square = lax.optimization_barrier(jnp.mean(propagated * propagated, axis=(1, 2)))
    current = propagated / jnp.sqrt(mean_square + epsilon)[:, None, None]
    for repeat_index in range(NS_ITERS):
        intersection = jnp.einsum('wjp,wkp->wjk', current, current, precision=lax.Precision.HIGHEST) / NORB
        current = 0.5 * (3.0 * current - jnp.einsum('wjk,wkp->wjp', intersection, current, precision=lax.Precision.HIGHEST))
    return (current, new_log_weights)
```

```python
import functools
import math

import jax
import jax.numpy as jnp
from jax import lax
from jax.experimental import pallas as pl
from jax.experimental.pallas import tpu as pltpu
from jax.sharding import PartitionSpec as P

NS_ITERS = 2

gradient_step = 0.25
energy_step = 0.002
epsilon = 1e-06

MESH = pl.DeviceIdType.MESH
UNROLL_LIMIT = 8


def dot(a, b):
    return lax.dot_general(a, b, (((1,), (0,)), ((), ())), preferred_element_type=jnp.float32)


def dot_t(a, b):
    return lax.dot_general(a, b, (((1,), (1,)), ((), ())), preferred_element_type=jnp.float32)


def each(count, body):
    if count <= UNROLL_LIMIT:
        order = [1, count - 1] + list(range(2, count - 1)) if count > 2 else list(range(1, count))
        for k in order:
            body(k)
    else:
        lax.fori_loop(1, count, lambda k, c: (body(k), c)[1], 0)


def kernel(
    n_vec, n_wlk,
    chol_hbm, orb_hbm, logw_ref, par_ref, prop_hbm,
    out_ref, outlog_ref,
    chol, orb, prop, propb, theta, gsend, grecv, esend, erecv, acc, eacc, pop, plog,
    load_sem, th_send, th_recv, g_send, g_recv, e_send, e_recv, p_send, p_recv, l_send, l_recv,
):
    me = lax.axis_index("vec")
    mw = lax.axis_index("wlk")
    occ, basis = orb.shape
    vecs = chol.shape[0] // occ
    scale = 1.0 / math.sqrt(vecs * n_vec)

    load_orb = pltpu.make_async_copy(orb_hbm, orb, load_sem.at[0])
    load_chol = pltpu.make_async_copy(chol_hbm, chol, load_sem.at[1])
    load_prop = pltpu.make_async_copy(prop_hbm, prop, load_sem.at[2])
    load_orb.start()
    load_chol.start()
    load_prop.start()

    barrier = pltpu.get_barrier_semaphore()

    def greet_vec(k):
        pl.semaphore_signal(
            barrier, inc=1, device_id={"vec": lax.rem(me + k, n_vec)}, device_id_type=MESH)

    def greet_wlk(k):
        pl.semaphore_signal(
            barrier, inc=1, device_id={"wlk": lax.rem(mw + k, n_wlk)}, device_id_type=MESH)

    each(n_vec, greet_vec)
    each(n_wlk, greet_wlk)
    load_orb.wait()
    theta[me] = orb[...].astype(jnp.bfloat16)
    pl.semaphore_wait(barrier, n_vec - 1 + n_wlk - 1)

    def theta_copy(k):
        return pltpu.make_async_remote_copy(
            src_ref=theta.at[me], dst_ref=theta.at[me],
            send_sem=th_send.at[k], recv_sem=th_recv.at[me],
            device_id={"vec": lax.rem(me + k, n_vec)}, device_id_type=MESH)

    def theta_arrival(src):
        return pltpu.make_async_remote_copy(
            src_ref=theta.at[src], dst_ref=theta.at[src],
            send_sem=th_send.at[0], recv_sem=th_recv.at[src],
            device_id={"vec": src}, device_id_type=MESH)

    if n_vec <= UNROLL_LIMIT:
        for k in list(range(2, n_vec - 1)) + [1] + ([n_vec - 1] if n_vec > 2 else []):
            theta_copy(k).start()
    else:
        each(n_vec, lambda k: theta_copy(k).start())

    load_chol.wait()
    row = lax.broadcasted_iota(jnp.int32, (occ, occ), 0)
    col = lax.broadcasted_iota(jnp.int32, (occ, occ), 1)
    diagonal = row == col

    def contribution(th):
        s = dot_t(chol[...], th)
        blocks = []
        exchange = jnp.zeros((occ, occ), jnp.float32)
        squares = jnp.zeros((1, 1), jnp.float32)
        for g in range(vecs):
            sg = s[g * occ:(g + 1) * occ, :]
            on_diagonal = jnp.where(diagonal, sg, 0.0)
            tg = jnp.sum(jnp.sum(on_diagonal, axis=0, keepdims=True), axis=1, keepdims=True)
            exchange = exchange + sg * sg.T
            squares = squares + tg * tg
            blocks.append((scale * (jnp.where(diagonal, tg, 0.0) - sg)).astype(jnp.bfloat16))
        adjoint = jnp.concatenate(blocks, axis=1)
        total = jnp.sum(jnp.sum(exchange, axis=0, keepdims=True), axis=1, keepdims=True)
        energy = 0.5 * scale * (squares - total)
        return dot(adjoint, chol[...]), jnp.broadcast_to(energy, (8, 128))

    gradient, energy = contribution(theta[me])
    acc[...] = gradient
    eacc[...] = energy

    load_prop.wait()
    propb[...] = prop[...].astype(jnp.bfloat16)

    def gradient_copy(k, dst):
        return pltpu.make_async_remote_copy(
            src_ref=gsend.at[k], dst_ref=grecv.at[me],
            send_sem=g_send.at[k], recv_sem=g_recv.at[me],
            device_id={"vec": dst}, device_id_type=MESH)

    def energy_copy(k, dst):
        return pltpu.make_async_remote_copy(
            src_ref=esend.at[k], dst_ref=erecv.at[me],
            send_sem=e_send.at[k], recv_sem=e_recv.at[me],
            device_id={"vec": dst}, device_id_type=MESH)

    def serve(k):
        src = lax.rem(me + k, n_vec)
        theta_arrival(src).wait_recv()
        gradient, energy = contribution(theta[src])
        esend[k] = energy
        gsend[k] = gradient.astype(jnp.bfloat16)
        gradient_copy(k, src).start()
        energy_copy(k, src).start()

    each(n_vec, serve)

    def collect(k):
        src = lax.rem(me + k, n_vec)
        pltpu.make_async_remote_copy(
            src_ref=gsend.at[0], dst_ref=grecv.at[src],
            send_sem=g_send.at[0], recv_sem=g_recv.at[src],
            device_id={"vec": src}, device_id_type=MESH).wait_recv()
        pltpu.make_async_remote_copy(
            src_ref=esend.at[0], dst_ref=erecv.at[src],
            send_sem=e_send.at[0], recv_sem=e_recv.at[src],
            device_id={"vec": src}, device_id_type=MESH).wait_recv()
        acc[...] += grecv[src].astype(jnp.float32)
        eacc[...] += erecv[src]

    each(n_vec, collect)

    pop[mw] = (orb[...] - gradient_step * acc[...]).astype(jnp.bfloat16)
    plog[mw] = logw_ref[0] - energy_step * eacc[...]

    def walker_copy(k):
        return pltpu.make_async_remote_copy(
            src_ref=pop.at[mw], dst_ref=pop.at[mw],
            send_sem=p_send.at[k], recv_sem=p_recv.at[mw],
            device_id={"wlk": lax.rem(mw + k, n_wlk)}, device_id_type=MESH)

    def log_copy(k):
        return pltpu.make_async_remote_copy(
            src_ref=plog.at[mw], dst_ref=plog.at[mw],
            send_sem=l_send.at[k], recv_sem=l_recv.at[mw],
            device_id={"wlk": lax.rem(mw + k, n_wlk)}, device_id_type=MESH)

    each(n_wlk, lambda k: walker_copy(k).start())
    each(n_wlk, lambda k: log_copy(k).start())

    def arrive(k):
        src = lax.rem(mw + k, n_wlk)
        pltpu.make_async_remote_copy(
            src_ref=pop.at[src], dst_ref=pop.at[src],
            send_sem=p_send.at[0], recv_sem=p_recv.at[src],
            device_id={"wlk": src}, device_id_type=MESH).wait_recv()
        pltpu.make_async_remote_copy(
            src_ref=plog.at[src], dst_ref=plog.at[src],
            send_sem=l_send.at[0], recv_sem=l_recv.at[src],
            device_id={"wlk": src}, device_id_type=MESH).wait_recv()

    each(n_wlk, arrive)

    parent = par_ref[0]
    chosen = pop[0]
    chosen_log = plog[0]
    for k in range(1, n_wlk):
        chosen = jnp.where(parent == k, pop[k], chosen)
        chosen_log = jnp.where(parent == k, plog[k], chosen_log)
    outlog_ref[0] = jnp.max(chosen_log)

    x = dot_t(chosen, propb[...])
    mean_square = jnp.sum(jnp.sum(x * x, axis=0, keepdims=True), axis=1, keepdims=True)
    mean_square = mean_square / (occ * basis)
    x = x * (1.0 / jnp.sqrt(mean_square + epsilon))
    for _ in range(NS_ITERS):
        xb = x.astype(jnp.bfloat16)
        inter = (dot_t(xb, xb) / basis).astype(jnp.bfloat16)
        x = 0.5 * (3.0 * x - dot(inter, xb))
    out_ref[...] = x

    def drain_vec(k):
        theta_copy(k).wait_send()
        gradient_copy(k, me).wait_send()
        energy_copy(k, me).wait_send()

    def drain_wlk(k):
        walker_copy(k).wait_send()
        log_copy(k).wait_send()

    each(n_vec, drain_vec)
    each(n_wlk, drain_wlk)


def solution(mesh):
    n_vec, n_wlk = mesh.shape["vec"], mesh.shape["wlk"]

    def local(cholesky, orbitals, log_weights, parents, propagator):
        walkers, occ, basis = orbitals.shape
        assert walkers == 1
        vecs = cholesky.shape[0]
        f32, bf16 = jnp.float32, jnp.bfloat16
        dma = pltpu.SemaphoreType.DMA
        hbm = pl.BlockSpec(memory_space=pl.ANY)
        smem = pl.BlockSpec(memory_space=pltpu.SMEM)
        out, logs = pl.pallas_call(
            functools.partial(kernel, n_vec, n_wlk),
            out_shape=(
                jax.ShapeDtypeStruct((occ, basis), f32),
                jax.ShapeDtypeStruct((1,), f32),
            ),
            in_specs=[hbm, hbm, smem, smem, hbm],
            out_specs=(pl.BlockSpec(memory_space=pltpu.VMEM), smem),
            scratch_shapes=[
                pltpu.VMEM((vecs * occ, basis), bf16),
                pltpu.VMEM((occ, basis), f32),
                pltpu.VMEM(propagator.shape, f32),
                pltpu.VMEM(propagator.shape, bf16),
                pltpu.VMEM((n_vec, occ, basis), bf16),
                pltpu.VMEM((n_vec, occ, basis), bf16),
                pltpu.VMEM((n_vec, occ, basis), bf16),
                pltpu.VMEM((n_vec, 8, 128), f32),
                pltpu.VMEM((n_vec, 8, 128), f32),
                pltpu.VMEM((occ, basis), f32),
                pltpu.VMEM((8, 128), f32),
                pltpu.VMEM((n_wlk, occ, basis), bf16),
                pltpu.VMEM((n_wlk, 8, 128), f32),
                dma((3,)),
                dma((n_vec,)), dma((n_vec,)),
                dma((n_vec,)), dma((n_vec,)),
                dma((n_vec,)), dma((n_vec,)),
                dma((n_wlk,)), dma((n_wlk,)),
                dma((n_wlk,)), dma((n_wlk,)),
            ],
            compiler_params=pltpu.CompilerParams(
                collective_id=0, has_side_effects=True, vmem_limit_bytes=48 * 1024 * 1024),
        )(
            cholesky.reshape(vecs * occ, basis),
            orbitals.reshape(occ, basis),
            log_weights,
            parents,
            propagator,
        )
        return out.reshape(orbitals.shape), logs

    placed = (
        P(("grp", "vec"), None, None),
        P(("grp", "vec", "wlk"), None, None),
        P(("grp", "vec", "wlk")),
        P(("grp", "vec", "wlk")),
        P("grp", None),
    )
    return jax.shard_map(
        local,
        mesh=mesh,
        in_specs=placed,
        out_specs=(P(("grp", "vec", "wlk"), None, None), P(("grp", "vec", "wlk"))),
        check_vma=False,
    )
```

```python
import functools
import math

import jax
import jax.numpy as jnp
from jax import lax
from jax.experimental import pallas as pl
from jax.experimental.pallas import tpu as pltpu
from jax.sharding import PartitionSpec as P

NS_ITERS = 2

gradient_step = 0.25
energy_step = 0.002
epsilon = 1e-06

MESH = pl.DeviceIdType.MESH
UNROLL_LIMIT = 8
CHUNKS = 2


def dot(a, b):
    return lax.dot_general(a, b, (((1,), (0,)), ((), ())), preferred_element_type=jnp.float32)


def dot_t(a, b):
    return lax.dot_general(a, b, (((1,), (1,)), ((), ())), preferred_element_type=jnp.float32)


def each(count, body):
    if count <= UNROLL_LIMIT:
        for j in range(count):
            body(j)
    else:
        lax.fori_loop(0, count, lambda j, c: (body(j), c)[1], 0)


def by_distance(me, n, j):
    side = lax.div(2 * me, n)
    near = me + side * (n - 1 - 2 * me)
    spot = n - 1 - j - lax.div(near + j + 1, n)
    return spot + side * (n - 1 - 2 * spot)


def by_chip(me, n, j):
    if n % 2:
        return lax.rem(me + 1 + j, n)
    step = j + 2
    core = lax.rem(me + lax.rem(step, 2) + lax.div(step, n), 2)
    return lax.rem((lax.div(me, 2) + lax.div(step, 2)) * 2 + core, n)


def kernel(
    n_vec, n_wlk, chunks,
    chol_hbm, orb_hbm, logw_hbm, par_hbm, prop_hbm,
    out_ref, outlog_ref,
    logw, par, chol, orb, prop, propb, pop, plog, theta, gsend, grecv, esend, erecv, acc, eacc,
    load_sem, th_send, th_recv, g_send, g_recv, e_send, e_recv, p_send, p_recv, l_send, l_recv,
):
    me = lax.axis_index("vec")
    mw = lax.axis_index("wlk")
    occ, basis = orb.shape
    vecs = chol.shape[0] // occ
    scale = 1.0 / math.sqrt(vecs * n_vec)
    rows = occ // chunks

    loads = [
        pltpu.make_async_copy(src, dst, load_sem.at[i])
        for i, (src, dst) in enumerate((
            (orb_hbm, orb), (par_hbm, par), (logw_hbm, logw), (chol_hbm, chol), (prop_hbm, prop)))
    ]
    for load in loads:
        load.start()
    load_orb, load_par, load_logw, load_chol, load_prop = loads

    barrier = pltpu.get_barrier_semaphore()

    def greet_vec(j):
        pl.semaphore_signal(
            barrier, inc=1, device_id={"vec": by_distance(me, n_vec, j)}, device_id_type=MESH)

    def greet_wlk(j):
        pl.semaphore_signal(
            barrier, inc=1, device_id={"wlk": by_chip(mw, n_wlk, j)}, device_id_type=MESH)

    each(n_vec - 1, greet_vec)
    each(n_wlk - 1, greet_wlk)
    load_orb.wait()
    pop[mw] = orb[...].astype(jnp.bfloat16)
    load_logw.wait()
    plog[mw] = jnp.full((8, 128), logw[0], jnp.float32)
    load_par.wait()
    parent = par[0]
    pl.semaphore_wait(barrier, n_vec - 1 + n_wlk - 1)

    def walker_copy(h, src, dst):
        part = pl.ds(h * rows, rows)
        return pltpu.make_async_remote_copy(
            src_ref=pop.at[src, part], dst_ref=pop.at[src, part],
            send_sem=p_send.at[h, dst], recv_sem=p_recv.at[h, src],
            device_id={"wlk": dst}, device_id_type=MESH)

    def log_copy(src, dst):
        return pltpu.make_async_remote_copy(
            src_ref=plog.at[src], dst_ref=plog.at[src],
            send_sem=l_send.at[dst], recv_sem=l_recv.at[src],
            device_id={"wlk": dst}, device_id_type=MESH)

    def theta_copy(h, src, dst):
        part = pl.ds(h * rows, rows)
        return pltpu.make_async_remote_copy(
            src_ref=theta.at[src, part], dst_ref=theta.at[src, part],
            send_sem=th_send.at[h, dst], recv_sem=th_recv.at[h, src],
            device_id={"vec": dst}, device_id_type=MESH)

    def gradient_copy(src, dst):
        return pltpu.make_async_remote_copy(
            src_ref=gsend.at[dst], dst_ref=grecv.at[src],
            send_sem=g_send.at[dst], recv_sem=g_recv.at[src],
            device_id={"vec": dst}, device_id_type=MESH)

    def energy_copy(src, dst):
        return pltpu.make_async_remote_copy(
            src_ref=esend.at[dst], dst_ref=erecv.at[src],
            send_sem=e_send.at[dst], recv_sem=e_recv.at[src],
            device_id={"vec": dst}, device_id_type=MESH)

    for h in range(chunks):
        each(n_wlk - 1, lambda j: walker_copy(h, mw, by_chip(mw, n_wlk, j)).start())
    each(n_wlk - 1, lambda j: log_copy(mw, by_chip(mw, n_wlk, j)).start())

    for h in range(chunks):
        def arrive(j):
            src = by_chip(mw, n_wlk, n_wlk - 2 - j)
            walker_copy(h, src, mw).wait_recv()

        each(n_wlk - 1, arrive)
        part = pl.ds(h * rows, rows)
        chosen = pop[0, part]
        for k in range(1, n_wlk):
            chosen = jnp.where(parent == k, pop[k, part], chosen)
        theta[me, part] = chosen
        each(n_vec - 1, lambda j: theta_copy(h, me, by_distance(me, n_vec, j)).start())

    load_chol.wait()
    row = lax.broadcasted_iota(jnp.int32, (occ, occ), 0)
    col = lax.broadcasted_iota(jnp.int32, (occ, occ), 1)
    diagonal = row == col

    def contribution(th):
        s = dot_t(chol[...], th)
        blocks = []
        exchange = jnp.zeros((occ, occ), jnp.float32)
        squares = jnp.zeros((1, 1), jnp.float32)
        for g in range(vecs):
            sg = s[g * occ:(g + 1) * occ, :]
            on_diagonal = jnp.where(diagonal, sg, 0.0)
            tg = jnp.sum(jnp.sum(on_diagonal, axis=0, keepdims=True), axis=1, keepdims=True)
            exchange = exchange + sg * sg.T
            squares = squares + tg * tg
            blocks.append((scale * (jnp.where(diagonal, tg, 0.0) - sg)).astype(jnp.bfloat16))
        adjoint = jnp.concatenate(blocks, axis=1)
        total = jnp.sum(jnp.sum(exchange, axis=0, keepdims=True), axis=1, keepdims=True)
        energy = 0.5 * scale * (squares - total)
        return dot(adjoint, chol[...]), jnp.broadcast_to(energy, (8, 128))

    gradient, energy = contribution(theta[me])
    acc[...] = gradient
    eacc[...] = energy

    load_prop.wait()
    propb[...] = prop[...].astype(jnp.bfloat16)

    def serve(j):
        src = by_distance(me, n_vec, n_vec - 2 - j)
        for h in range(chunks):
            theta_copy(h, src, me).wait_recv()
        gradient, energy = contribution(theta[src])
        gsend[src] = gradient.astype(jnp.bfloat16)
        gradient_copy(me, src).start()
        esend[src] = energy
        energy_copy(me, src).start()

    each(n_vec - 1, serve)

    def log_arrive(j):
        log_copy(by_chip(mw, n_wlk, j), mw).wait_recv()

    each(n_wlk - 1, log_arrive)
    chosen_log = plog[0]
    for k in range(1, n_wlk):
        chosen_log = jnp.where(parent == k, plog[k], chosen_log)

    def collect(j):
        src = by_distance(me, n_vec, n_vec - 2 - j)
        gradient_copy(src, me).wait_recv()
        acc[...] += grecv[src].astype(jnp.float32)

    def collect_energy(j):
        src = by_distance(me, n_vec, n_vec - 2 - j)
        energy_copy(src, me).wait_recv()
        eacc[...] += erecv[src]

    each(n_vec - 1, collect)

    stepped = theta[me].astype(jnp.float32) - gradient_step * acc[...]
    x = dot_t(stepped.astype(jnp.bfloat16), propb[...])
    mean_square = jnp.sum(jnp.sum(x * x, axis=0, keepdims=True), axis=1, keepdims=True)
    mean_square = mean_square / (occ * basis)
    x = x * (1.0 / jnp.sqrt(mean_square + epsilon))
    for _ in range(NS_ITERS):
        xb = x.astype(jnp.bfloat16)
        inter = (dot_t(xb, xb) / basis).astype(jnp.bfloat16)
        x = 0.5 * (3.0 * x - dot(inter, xb))
    out_ref[...] = x

    each(n_vec - 1, collect_energy)
    outlog_ref[0] = jnp.max(chosen_log - energy_step * eacc[...])

    def drain_vec(j):
        dst = by_distance(me, n_vec, j)
        for h in range(chunks):
            theta_copy(h, me, dst).wait_send()
        gradient_copy(me, dst).wait_send()
        energy_copy(me, dst).wait_send()

    def drain_wlk(j):
        dst = by_chip(mw, n_wlk, j)
        for h in range(chunks):
            walker_copy(h, mw, dst).wait_send()
        log_copy(mw, dst).wait_send()

    each(n_vec - 1, drain_vec)
    each(n_wlk - 1, drain_wlk)


def solution(mesh):
    n_vec, n_wlk = mesh.shape["vec"], mesh.shape["wlk"]

    def local(cholesky, orbitals, log_weights, parents, propagator):
        walkers, occ, basis = orbitals.shape
        assert walkers == 1
        vecs = cholesky.shape[0]
        f32, bf16 = jnp.float32, jnp.bfloat16
        dma = pltpu.SemaphoreType.DMA
        hbm = pl.BlockSpec(memory_space=pltpu.HBM)
        smem = pl.BlockSpec(memory_space=pltpu.SMEM)
        out, logs = pl.pallas_call(
            functools.partial(kernel, n_vec, n_wlk, CHUNKS),
            out_shape=(
                jax.ShapeDtypeStruct((occ, basis), f32),
                jax.ShapeDtypeStruct((1,), f32),
            ),
            in_specs=[hbm] * 5,
            out_specs=(pl.BlockSpec(memory_space=pltpu.VMEM), smem),
            scratch_shapes=[
                pltpu.SMEM((1,), f32),
                pltpu.SMEM((1,), jnp.int32),
                pltpu.VMEM((vecs * occ, basis), bf16),
                pltpu.VMEM((occ, basis), f32),
                pltpu.VMEM(propagator.shape, f32),
                pltpu.VMEM(propagator.shape, bf16),
                pltpu.VMEM((n_wlk, occ, basis), bf16),
                pltpu.VMEM((n_wlk, 8, 128), f32),
                pltpu.VMEM((n_vec, occ, basis), bf16),
                pltpu.VMEM((n_vec, occ, basis), bf16),
                pltpu.VMEM((n_vec, occ, basis), bf16),
                pltpu.VMEM((n_vec, 8, 128), f32),
                pltpu.VMEM((n_vec, 8, 128), f32),
                pltpu.VMEM((occ, basis), f32),
                pltpu.VMEM((8, 128), f32),
                dma((5,)),
                dma((CHUNKS, n_vec)), dma((CHUNKS, n_vec)),
                dma((n_vec,)), dma((n_vec,)),
                dma((n_vec,)), dma((n_vec,)),
                dma((CHUNKS, n_wlk)), dma((CHUNKS, n_wlk)),
                dma((n_wlk,)), dma((n_wlk,)),
            ],
            compiler_params=pltpu.CompilerParams(
                collective_id=0, has_side_effects=True, vmem_limit_bytes=48 * 1024 * 1024),
        )(
            cholesky.reshape(vecs * occ, basis),
            orbitals.reshape(occ, basis),
            log_weights,
            parents,
            propagator,
        )
        return out.reshape(orbitals.shape), logs

    placed = (
        P(("grp", "vec"), None, None),
        P(("grp", "vec", "wlk"), None, None),
        P(("grp", "vec", "wlk")),
        P(("grp", "vec", "wlk")),
        P("grp", None),
    )
    return jax.shard_map(
        local,
        mesh=mesh,
        in_specs=placed,
        out_specs=(P(("grp", "vec", "wlk"), None, None), P(("grp", "vec", "wlk"))),
        check_vma=False,
    )
```

```python
import functools
import math

import jax
import jax.numpy as jnp
from jax import lax
from jax.experimental import pallas as pl
from jax.experimental.pallas import tpu as pltpu
from jax.sharding import PartitionSpec as P

NS_ITERS = 2

gradient_step = 0.25
energy_step = 0.002
epsilon = 1e-06

MESH = pl.DeviceIdType.MESH
UNROLL_LIMIT = 8
CHUNKS = 2


def dot(a, b):
    return lax.dot_general(a, b, (((1,), (0,)), ((), ())), preferred_element_type=jnp.float32)


def dot_t(a, b):
    return lax.dot_general(a, b, (((1,), (1,)), ((), ())), preferred_element_type=jnp.float32)


def each(count, body):
    if count <= UNROLL_LIMIT:
        for j in range(count):
            body(j)
    else:
        lax.fori_loop(0, count, lambda j, c: (body(j), c)[1], 0)


def by_distance(me, n, j):
    side = lax.div(2 * me, n)
    near = me + side * (n - 1 - 2 * me)
    spot = n - 1 - j - lax.div(near + j + 1, n)
    return spot + side * (n - 1 - 2 * spot)


def by_chip(me, n, j):
    if n % 2:
        return lax.rem(me + 1 + j, n)
    step = j + 2
    core = lax.rem(me + lax.rem(step, 2) + lax.div(step, n), 2)
    return lax.rem((lax.div(me, 2) + lax.div(step, 2)) * 2 + core, n)


def kernel(
    n_vec, n_wlk, chunks,
    chol_hbm, orb_hbm, logw_hbm, par_hbm, prop_hbm,
    out_ref, outlog_ref,
    logw, par, chol, orb, prop, propb, pop, plog, theta, gsend, grecv, esend, erecv, acc, eacc,
    load_sem, th_send, th_recv, g_send, g_recv, e_send, e_recv, p_send, p_recv, l_send, l_recv,
):
    me = lax.axis_index("vec")
    mw = lax.axis_index("wlk")
    occ, basis = orb.shape
    vecs = chol.shape[0] // occ
    scale = 1.0 / math.sqrt(vecs * n_vec)
    rows = occ // chunks

    loads = [
        pltpu.make_async_copy(src, dst, load_sem.at[i])
        for i, (src, dst) in enumerate((
            (orb_hbm, orb), (par_hbm, par), (logw_hbm, logw), (chol_hbm, chol), (prop_hbm, prop)))
    ]
    for load in loads:
        load.start()
    load_orb, load_par, load_logw, load_chol, load_prop = loads

    barrier = pltpu.get_barrier_semaphore()

    def greet_vec(j):
        pl.semaphore_signal(
            barrier, inc=1, device_id={"vec": by_distance(me, n_vec, j)}, device_id_type=MESH)

    def greet_wlk(j):
        pl.semaphore_signal(
            barrier, inc=1, device_id={"wlk": by_chip(mw, n_wlk, j)}, device_id_type=MESH)

    each(n_vec - 1, greet_vec)
    each(n_wlk - 1, greet_wlk)
    load_orb.wait()
    pop[mw] = orb[...].astype(jnp.bfloat16)
    load_logw.wait()
    plog[mw] = jnp.full((8, 128), logw[0], jnp.float32)
    load_par.wait()
    parent = par[0]
    pl.semaphore_wait(barrier, n_vec - 1 + n_wlk - 1)

    def walker_copy(h, src, dst):
        part = pl.ds(h * rows, rows)
        return pltpu.make_async_remote_copy(
            src_ref=pop.at[src, part], dst_ref=pop.at[src, part],
            send_sem=p_send.at[h, dst], recv_sem=p_recv.at[h, src],
            device_id={"wlk": dst}, device_id_type=MESH)

    def log_copy(src, dst):
        return pltpu.make_async_remote_copy(
            src_ref=plog.at[src], dst_ref=plog.at[src],
            send_sem=l_send.at[dst], recv_sem=l_recv.at[src],
            device_id={"wlk": dst}, device_id_type=MESH)

    def theta_copy(h, src, dst):
        part = pl.ds(h * rows, rows)
        return pltpu.make_async_remote_copy(
            src_ref=theta.at[src, part], dst_ref=theta.at[src, part],
            send_sem=th_send.at[h, dst], recv_sem=th_recv.at[h, src],
            device_id={"vec": dst}, device_id_type=MESH)

    def gradient_copy(src, dst):
        return pltpu.make_async_remote_copy(
            src_ref=gsend.at[dst], dst_ref=grecv.at[src],
            send_sem=g_send.at[dst], recv_sem=g_recv.at[src],
            device_id={"vec": dst}, device_id_type=MESH)

    def energy_copy(src, dst):
        return pltpu.make_async_remote_copy(
            src_ref=esend.at[dst], dst_ref=erecv.at[src],
            send_sem=e_send.at[dst], recv_sem=e_recv.at[src],
            device_id={"vec": dst}, device_id_type=MESH)

    for h in range(chunks):
        each(n_wlk - 1, lambda j: walker_copy(h, mw, by_chip(mw, n_wlk, j)).start())
    each(n_wlk - 1, lambda j: log_copy(mw, by_chip(mw, n_wlk, j)).start())

    for h in range(chunks):
        def arrive(j):
            src = by_chip(mw, n_wlk, n_wlk - 2 - j)
            walker_copy(h, src, mw).wait_recv()

        each(n_wlk - 1, arrive)
        part = pl.ds(h * rows, rows)
        chosen = pop[0, part]
        for k in range(1, n_wlk):
            chosen = jnp.where(parent == k, pop[k, part], chosen)
        theta[me, part] = chosen
        each(n_vec - 1, lambda j: theta_copy(h, me, by_distance(me, n_vec, j)).start())

    load_chol.wait()
    row = lax.broadcasted_iota(jnp.int32, (occ, occ), 0)
    col = lax.broadcasted_iota(jnp.int32, (occ, occ), 1)
    diagonal = row == col

    def contribution(th):
        s = dot_t(chol[...], th)
        blocks = []
        exchange = jnp.zeros((occ, occ), jnp.float32)
        squares = jnp.zeros((1, 1), jnp.float32)
        for g in range(vecs):
            sg = s[g * occ:(g + 1) * occ, :]
            on_diagonal = jnp.where(diagonal, sg, 0.0)
            tg = jnp.sum(jnp.sum(on_diagonal, axis=0, keepdims=True), axis=1, keepdims=True)
            exchange = exchange + sg * sg.T
            squares = squares + tg * tg
            blocks.append((scale * (jnp.where(diagonal, tg, 0.0) - sg)).astype(jnp.bfloat16))
        adjoint = jnp.concatenate(blocks, axis=1)
        total = jnp.sum(jnp.sum(exchange, axis=0, keepdims=True), axis=1, keepdims=True)
        energy = 0.5 * scale * (squares - total)
        return dot(adjoint, chol[...]), jnp.broadcast_to(energy, (8, 128))

    gradient, energy = contribution(theta[me])
    acc[...] = gradient
    eacc[...] = energy

    load_prop.wait()
    propb[...] = prop[...].astype(jnp.bfloat16)

    def serve(j):
        src = by_distance(me, n_vec, n_vec - 2 - j)
        for h in range(chunks):
            theta_copy(h, src, me).wait_recv()
        gradient, energy = contribution(theta[src])
        gsend[src] = gradient.astype(jnp.bfloat16)
        gradient_copy(me, src).start()
        esend[src] = energy
        energy_copy(me, src).start()

    each(n_vec - 1, serve)

    def log_arrive(j):
        log_copy(by_chip(mw, n_wlk, j), mw).wait_recv()

    each(n_wlk - 1, log_arrive)
    chosen_log = plog[0]
    for k in range(1, n_wlk):
        chosen_log = jnp.where(parent == k, plog[k], chosen_log)

    def collect(j):
        src = by_distance(me, n_vec, n_vec - 2 - j)
        gradient_copy(src, me).wait_recv()
        acc[...] += grecv[src].astype(jnp.float32)

    def collect_energy(j):
        src = by_distance(me, n_vec, n_vec - 2 - j)
        energy_copy(src, me).wait_recv()
        eacc[...] += erecv[src]

    each(n_vec - 1, collect)

    stepped = theta[me].astype(jnp.float32) - gradient_step * acc[...]
    x = dot_t(stepped.astype(jnp.bfloat16), propb[...])
    mean_square = jnp.sum(jnp.sum(x * x, axis=0, keepdims=True), axis=1, keepdims=True)
    mean_square = mean_square / (occ * basis)
    x = x * (1.0 / jnp.sqrt(mean_square + epsilon))
    for _ in range(NS_ITERS):
        xb = x.astype(jnp.bfloat16)
        inter = (dot_t(xb, xb) / basis).astype(jnp.bfloat16)
        x = 0.5 * (3.0 * x - dot(inter, xb))
    out_ref[...] = x

    each(n_vec - 1, collect_energy)
    outlog_ref[0] = jnp.max(chosen_log - energy_step * eacc[...])

    def drain_vec(j):
        dst = by_distance(me, n_vec, j)
        for h in range(chunks):
            theta_copy(h, me, dst).wait_send()
        gradient_copy(me, dst).wait_send()
        energy_copy(me, dst).wait_send()

    def drain_wlk(j):
        dst = by_chip(mw, n_wlk, j)
        for h in range(chunks):
            walker_copy(h, mw, dst).wait_send()
        log_copy(mw, dst).wait_send()

    each(n_vec - 1, drain_vec)
    each(n_wlk - 1, drain_wlk)


def solution(mesh):
    n_vec, n_wlk = mesh.shape["vec"], mesh.shape["wlk"]

    def local(cholesky, orbitals, log_weights, parents, propagator):
        walkers, occ, basis = orbitals.shape
        assert walkers == 1
        vecs = cholesky.shape[0]
        f32, bf16 = jnp.float32, jnp.bfloat16
        dma = pltpu.SemaphoreType.DMA
        hbm = pl.BlockSpec(memory_space=pltpu.HBM)
        smem = pl.BlockSpec(memory_space=pltpu.SMEM)
        out, logs = pl.pallas_call(
            functools.partial(kernel, n_vec, n_wlk, CHUNKS),
            out_shape=(
                jax.ShapeDtypeStruct((occ, basis), f32),
                jax.ShapeDtypeStruct((1,), f32),
            ),
            in_specs=[hbm] * 5,
            out_specs=(pl.BlockSpec(memory_space=pltpu.VMEM), smem),
            scratch_shapes=[
                pltpu.SMEM((1,), f32),
                pltpu.SMEM((1,), jnp.int32),
                pltpu.VMEM((vecs * occ, basis), bf16),
                pltpu.VMEM((occ, basis), f32),
                pltpu.VMEM(propagator.shape, f32),
                pltpu.VMEM(propagator.shape, bf16),
                pltpu.VMEM((n_wlk, occ, basis), bf16),
                pltpu.VMEM((n_wlk, 8, 128), f32),
                pltpu.VMEM((n_vec, occ, basis), bf16),
                pltpu.VMEM((n_vec, occ, basis), bf16),
                pltpu.VMEM((n_vec, occ, basis), bf16),
                pltpu.VMEM((n_vec, 8, 128), f32),
                pltpu.VMEM((n_vec, 8, 128), f32),
                pltpu.VMEM((occ, basis), f32),
                pltpu.VMEM((8, 128), f32),
                dma((5,)),
                dma((CHUNKS, n_vec)), dma((CHUNKS, n_vec)),
                dma((n_vec,)), dma((n_vec,)),
                dma((n_vec,)), dma((n_vec,)),
                dma((CHUNKS, n_wlk)), dma((CHUNKS, n_wlk)),
                dma((n_wlk,)), dma((n_wlk,)),
            ],
            compiler_params=pltpu.CompilerParams(
                collective_id=0, has_side_effects=True, vmem_limit_bytes=67043328),
        )(
            cholesky.reshape(vecs * occ, basis),
            orbitals.reshape(occ, basis),
            log_weights,
            parents,
            propagator,
        )
        return out.reshape(orbitals.shape), logs

    placed = (
        P(("grp", "vec"), None, None),
        P(("grp", "vec", "wlk"), None, None),
        P(("grp", "vec", "wlk")),
        P(("grp", "vec", "wlk")),
        P("grp", None),
    )
    return jax.shard_map(
        local,
        mesh=mesh,
        in_specs=placed,
        out_specs=(P(("grp", "vec", "wlk"), None, None), P(("grp", "vec", "wlk"))),
        check_vma=False,
    )
```

```python
import functools
import math

import jax
import jax.numpy as jnp
from jax import lax
from jax.experimental import pallas as pl
from jax.experimental.pallas import tpu as pltpu
from jax.sharding import PartitionSpec as P

NS_ITERS = 2

gradient_step = 0.25
energy_step = 0.002
epsilon = 1e-06

MESH = pl.DeviceIdType.MESH
UNROLL_LIMIT = 8


def dot(a, b):
    return lax.dot_general(a, b, (((1,), (0,)), ((), ())), preferred_element_type=jnp.float32)


def dot_t(a, b):
    return lax.dot_general(a, b, (((1,), (1,)), ((), ())), preferred_element_type=jnp.float32)


def each(count, body):
    if count <= UNROLL_LIMIT:
        for j in range(count):
            body(j)
    else:
        lax.fori_loop(0, count, lambda j, c: (body(j), c)[1], 0)


def by_distance(me, n, j):
    side = lax.div(2 * me, n)
    near = me + side * (n - 1 - 2 * me)
    spot = n - 1 - j - lax.div(near + j + 1, n)
    return spot + side * (n - 1 - 2 * spot)


def by_chip(me, n, j):
    if n % 2:
        return lax.rem(me + 1 + j, n)
    step = j + 2
    core = lax.rem(me + lax.rem(step, 2) + lax.div(step, n), 2)
    return lax.rem((lax.div(me, 2) + lax.div(step, 2)) * 2 + core, n)


def kernel(
    n_vec, n_wlk, vecs,
    chol_hbm, orb_hbm, logw_hbm, par_hbm, prop_hbm,
    out_ref, outlog_ref,
    logw, par, orb, prop, propb, pop, tile, chosen, shared, gsend, grecv, esend, erecv, acc, eacc,
    load_sem, c_load, c_send, c_recv, p_send, p_recv, t_send, t_recv,
    g_send, g_recv, e_send, e_recv,
):
    me = lax.axis_index("vec")
    mw = lax.axis_index("wlk")
    occ, basis = orb.shape
    slots = shared.shape[1] // occ
    scale = 1.0 / math.sqrt(vecs * n_vec)
    others, peers = n_vec - 1, n_wlk - 1

    half = n_wlk // 2
    place = lax.rem(mw, 2) * half + lax.div(mw, 2) if n_wlk % 2 == 0 else mw

    def in_slot(slot, body):
        if (slot + 1) * n_wlk <= vecs:
            body()
        else:
            pl.when(slot * n_wlk + place < vecs)(body)

    def share(slot):
        return pl.ds(pl.multiple_of((slot * n_wlk + place) * occ, occ), occ)

    def spot(slot):
        return pl.ds(slot * occ, occ)

    def own_copy(slot):
        return pltpu.make_async_copy(
            chol_hbm.at[share(slot)], shared.at[me, spot(slot)], c_load.at[slot])

    def vector_copy(slot, src, dst):
        return pltpu.make_async_remote_copy(
            src_ref=chol_hbm.at[share(slot)], dst_ref=shared.at[src, spot(slot)],
            send_sem=c_send.at[slot, dst], recv_sem=c_recv.at[slot, src],
            device_id={"vec": dst}, device_id_type=MESH)

    def to_peer(src_ref, dst_ref, send, recv, dst):
        return pltpu.make_async_remote_copy(
            src_ref=src_ref, dst_ref=dst_ref, send_sem=send, recv_sem=recv,
            device_id={"wlk": dst}, device_id_type=MESH)

    def walker_copy(src, dst):
        return to_peer(pop.at[src], pop.at[src], p_send.at[dst], p_recv.at[src], dst)

    def tile_copy(src, dst):
        return to_peer(tile.at[src], tile.at[src], t_send.at[dst], t_recv.at[src], dst)

    def gradient_copy(src, dst):
        return to_peer(gsend.at[dst], grecv.at[src], g_send.at[dst], g_recv.at[src], dst)

    def energy_copy(src, dst):
        return to_peer(esend.at[dst], erecv.at[src], e_send.at[dst], e_recv.at[src], dst)

    loads = [
        pltpu.make_async_copy(src, dst, load_sem.at[i])
        for i, (src, dst) in enumerate((
            (orb_hbm, orb), (par_hbm, par), (logw_hbm, logw), (prop_hbm, prop)))
    ]
    for load in loads:
        load.start()
    load_orb, load_par, load_logw, load_prop = loads

    barrier = pltpu.get_barrier_semaphore()

    def greet_vec(j):
        pl.semaphore_signal(
            barrier, inc=1, device_id={"vec": by_distance(me, n_vec, j)}, device_id_type=MESH)

    def greet_wlk(j):
        pl.semaphore_signal(
            barrier, inc=1, device_id={"wlk": by_chip(mw, n_wlk, j)}, device_id_type=MESH)

    each(others, greet_vec)
    each(peers, greet_wlk)
    for slot in range(slots):
        in_slot(slot, lambda: own_copy(slot).start())
        if (slot + 1) * n_wlk > vecs:
            @pl.when(slot * n_wlk + place >= vecs)
            def _():
                shared[:, slot * occ:(slot + 1) * occ, :] = jnp.zeros(
                    (n_vec, occ, basis), jnp.bfloat16)
    load_orb.wait()
    pop[mw] = orb[...].astype(jnp.bfloat16)
    load_logw.wait()
    load_par.wait()
    tile[mw, 0:8] = jnp.broadcast_to(logw[...], (8, 128))
    tile[mw, 8:16] = jnp.broadcast_to(par[...], (8, 128)).astype(jnp.float32)
    pl.semaphore_wait(barrier, others + peers)

    for slot in range(slots):
        def send_vectors():
            each(others, lambda j: vector_copy(slot, me, by_distance(me, n_vec, j)).start())

        in_slot(slot, send_vectors)
    each(peers, lambda j: walker_copy(mw, by_chip(mw, n_wlk, j)).start())
    each(peers, lambda j: tile_copy(mw, by_chip(mw, n_wlk, j)).start())

    load_prop.wait()
    propb[...] = prop[...].astype(jnp.bfloat16)
    each(peers, lambda j: tile_copy(by_chip(mw, n_wlk, j), mw).wait_recv())
    each(peers, lambda j: walker_copy(by_chip(mw, n_wlk, j), mw).wait_recv())

    def pick(parent, read):
        value = read(0)
        for m in range(1, n_wlk):
            value = jnp.where(parent == m, read(m), value)
        return value

    for k in range(n_wlk):
        parent = jnp.broadcast_to(tile[k, 8:9, 0:1], (occ, basis))
        chosen[k] = pick(parent, lambda m: pop[m].astype(jnp.float32)).astype(jnp.bfloat16)
    chosen_log = pick(tile[mw, 8:16], lambda m: tile[m, 0:8])

    row = lax.broadcasted_iota(jnp.int32, (occ, occ), 0)
    col = lax.broadcasted_iota(jnp.int32, (occ, occ), 1)
    diagonal = row == col

    def contribution(source, first):
        vectors = shared[source]
        for k in range(n_wlk):
            s = dot_t(vectors, chosen[k])
            blocks = []
            exchange = jnp.zeros((occ, occ), jnp.float32)
            squares = jnp.zeros((1, 1), jnp.float32)
            for g in range(slots):
                sg = s[g * occ:(g + 1) * occ, :]
                on_diagonal = jnp.where(diagonal, sg, 0.0)
                tg = jnp.sum(jnp.sum(on_diagonal, axis=0, keepdims=True), axis=1, keepdims=True)
                exchange = exchange + sg * sg.T
                squares = squares + tg * tg
                blocks.append((scale * (jnp.where(diagonal, tg, 0.0) - sg)).astype(jnp.bfloat16))
            adjoint = jnp.concatenate(blocks, axis=1) if slots > 1 else blocks[0]
            total = jnp.sum(jnp.sum(exchange, axis=0, keepdims=True), axis=1, keepdims=True)
            energy = jnp.broadcast_to(0.5 * scale * (squares - total), (8, 128))
            gradient = dot(adjoint, vectors)
            if first:
                acc[k] = gradient
                eacc[k] = energy
            else:
                acc[k] += gradient
                eacc[k] += energy

    for slot in range(slots):
        in_slot(slot, lambda: own_copy(slot).wait())
    contribution(me, True)

    def serve(j):
        src = by_distance(me, n_vec, others - 1 - j)
        for slot in range(slots):
            in_slot(slot, lambda: vector_copy(slot, src, me).wait_recv())
        contribution(src, False)

    each(others, serve)

    def give(j):
        dst = by_chip(mw, n_wlk, j)
        gsend[dst] = acc[dst].astype(jnp.bfloat16)
        gradient_copy(mw, dst).start()
        esend[dst] = eacc[dst]
        energy_copy(mw, dst).start()

    each(peers, give)
    acc[mw] = chosen[mw].astype(jnp.float32) - gradient_step * acc[mw]

    def collect(j):
        src = by_chip(mw, n_wlk, peers - 1 - j)
        gradient_copy(src, mw).wait_recv()
        acc[mw] -= gradient_step * grecv[src].astype(jnp.float32)

    def collect_energy(j):
        src = by_chip(mw, n_wlk, peers - 1 - j)
        energy_copy(src, mw).wait_recv()
        eacc[mw] += erecv[src]

    each(peers, collect)

    x = dot_t(acc[mw].astype(jnp.bfloat16), propb[...])
    mean_square = jnp.sum(jnp.sum(x * x, axis=0, keepdims=True), axis=1, keepdims=True)
    mean_square = mean_square / (occ * basis)
    x = x * (1.0 / jnp.sqrt(mean_square + epsilon))
    for _ in range(NS_ITERS):
        xb = x.astype(jnp.bfloat16)
        inter = (dot_t(xb, xb) / basis).astype(jnp.bfloat16)
        x = 0.5 * (3.0 * x - dot(inter, xb))
    out_ref[...] = x

    each(peers, collect_energy)
    outlog_ref[0] = jnp.max(chosen_log - energy_step * eacc[mw])

    def drain_vec(j):
        dst = by_distance(me, n_vec, j)
        for slot in range(slots):
            in_slot(slot, lambda: vector_copy(slot, me, dst).wait_send())

    def drain_wlk(j):
        dst = by_chip(mw, n_wlk, j)
        walker_copy(mw, dst).wait_send()
        tile_copy(mw, dst).wait_send()
        gradient_copy(mw, dst).wait_send()
        energy_copy(mw, dst).wait_send()

    each(others, drain_vec)
    each(peers, drain_wlk)


def solution(mesh):
    n_vec, n_wlk = mesh.shape["vec"], mesh.shape["wlk"]

    def local(cholesky, orbitals, log_weights, parents, propagator):
        walkers, occ, basis = orbitals.shape
        assert walkers == 1
        vecs = cholesky.shape[0]
        slots = -(-vecs // n_wlk)
        f32, bf16 = jnp.float32, jnp.bfloat16
        dma = pltpu.SemaphoreType.DMA
        hbm = pl.BlockSpec(memory_space=pltpu.HBM)
        smem = pl.BlockSpec(memory_space=pltpu.SMEM)
        out, logs = pl.pallas_call(
            functools.partial(kernel, n_vec, n_wlk, vecs),
            out_shape=(
                jax.ShapeDtypeStruct((occ, basis), f32),
                jax.ShapeDtypeStruct((1,), f32),
            ),
            in_specs=[hbm] * 5,
            out_specs=(pl.BlockSpec(memory_space=pltpu.VMEM), smem),
            scratch_shapes=[
                pltpu.VMEM((1, 1), f32),
                pltpu.VMEM((1, 1), jnp.int32),
                pltpu.VMEM((occ, basis), f32),
                pltpu.VMEM(propagator.shape, f32),
                pltpu.VMEM(propagator.shape, bf16),
                pltpu.VMEM((n_wlk, occ, basis), bf16),
                pltpu.VMEM((n_wlk, 16, 128), f32),
                pltpu.VMEM((n_wlk, occ, basis), bf16),
                pltpu.VMEM((n_vec, slots * occ, basis), bf16),
                pltpu.VMEM((n_wlk, occ, basis), bf16),
                pltpu.VMEM((n_wlk, occ, basis), bf16),
                pltpu.VMEM((n_wlk, 8, 128), f32),
                pltpu.VMEM((n_wlk, 8, 128), f32),
                pltpu.VMEM((n_wlk, occ, basis), f32),
                pltpu.VMEM((n_wlk, 8, 128), f32),
                dma((4,)),
                dma((slots,)), dma((slots, n_vec)), dma((slots, n_vec)),
            ] + [dma((n_wlk,))] * 8,
            compiler_params=pltpu.CompilerParams(
                collective_id=0, has_side_effects=True, vmem_limit_bytes=67043328),
        )(
            cholesky.reshape(vecs * occ, basis),
            orbitals.reshape(occ, basis),
            log_weights.reshape(1, 1),
            parents.reshape(1, 1),
            propagator,
        )
        return out.reshape(orbitals.shape), logs

    placed = (
        P(("grp", "vec"), None, None),
        P(("grp", "vec", "wlk"), None, None),
        P(("grp", "vec", "wlk")),
        P(("grp", "vec", "wlk")),
        P("grp", None),
    )
    return jax.shard_map(
        local,
        mesh=mesh,
        in_specs=placed,
        out_specs=(P(("grp", "vec", "wlk"), None, None), P(("grp", "vec", "wlk"))),
        check_vma=False,
    )
```

```python
import functools
import math

import jax
import jax.numpy as jnp
from jax import lax
from jax.experimental import pallas as pl
from jax.experimental.pallas import tpu as pltpu
from jax.sharding import PartitionSpec as P

NS_ITERS = 2

gradient_step = 0.25
energy_step = 0.002
epsilon = 1e-06

MESH = pl.DeviceIdType.MESH
UNROLL_LIMIT = 8


def dot(a, b):
    return lax.dot_general(a, b, (((1,), (0,)), ((), ())), preferred_element_type=jnp.float32)


def dot_t(a, b):
    return lax.dot_general(a, b, (((1,), (1,)), ((), ())), preferred_element_type=jnp.float32)


def each(count, body):
    if count <= UNROLL_LIMIT:
        for j in range(count):
            body(j)
    else:
        lax.fori_loop(0, count, lambda j, c: (body(j), c)[1], 0)


def by_distance(me, n, j):
    side = lax.div(2 * me, n)
    near = me + side * (n - 1 - 2 * me)
    spot = n - 1 - j - lax.div(near + j + 1, n)
    return spot + side * (n - 1 - 2 * spot)


def by_chip(me, n, j):
    if n % 2:
        return lax.rem(me + 1 + j, n)
    step = j + 2
    core = lax.rem(me + lax.rem(step, 2) + lax.div(step, n), 2)
    return lax.rem((lax.div(me, 2) + lax.div(step, 2)) * 2 + core, n)


def kernel(
    n_vec, n_wlk, vecs,
    chol_hbm, orb_hbm, logw_hbm, par_hbm, prop_hbm,
    out_ref, outlog_ref,
    logw, par, orb, prop, propb, pop, tile, chosen, shared, gsend, grecv, esend, erecv, acc, eacc,
    load_sem, c_load, c_send, c_recv, r_send, p_send, p_recv, t_send, t_recv,
    g_send, g_recv, e_send, e_recv,
):
    me = lax.axis_index("vec")
    mw = lax.axis_index("wlk")
    occ, basis = orb.shape
    slots = shared.shape[1] // occ
    scale = 1.0 / math.sqrt(vecs * n_vec)
    others, peers = n_vec - 1, n_wlk - 1

    half = n_wlk // 2
    place = lax.rem(mw, 2) * half + lax.div(mw, 2) if n_wlk % 2 == 0 else mw

    def in_slot(slot, body):
        if (slot + 1) * n_wlk <= vecs:
            body()
        else:
            pl.when(slot * n_wlk + place < vecs)(body)

    def share(slot):
        return pl.ds(pl.multiple_of((slot * n_wlk + place) * occ, occ), occ)

    def spot(slot):
        return pl.ds(slot * occ, occ)

    def own_copy(slot):
        return pltpu.make_async_copy(
            chol_hbm.at[share(slot)], shared.at[me, spot(slot)], c_load.at[slot])

    def vector_copy(slot, src, dst):
        return pltpu.make_async_remote_copy(
            src_ref=chol_hbm.at[share(slot)], dst_ref=shared.at[src, spot(slot)],
            send_sem=c_send.at[slot, dst], recv_sem=c_recv.at[slot, src],
            device_id={"vec": dst}, device_id_type=MESH)

    side = lax.div(2 * me, n_vec)
    near = me + side * (n_vec - 1 - 2 * me)
    near_end, far_end = side * (n_vec - 1), n_vec - 1 - side * (n_vec - 1)
    relayed = n_vec >= 4

    def relay_copy(slot):
        return pltpu.make_async_remote_copy(
            src_ref=shared.at[far_end, spot(slot)], dst_ref=shared.at[far_end, spot(slot)],
            send_sem=r_send.at[slot], recv_sem=c_recv.at[slot, far_end],
            device_id={"vec": near_end}, device_id_type=MESH)

    def relay():
        for slot in range(slots):
            def forward():
                vector_copy(slot, far_end, me).wait_recv()
                relay_copy(slot).start()

            in_slot(slot, forward)

    def to_peer(src_ref, dst_ref, send, recv, dst):
        return pltpu.make_async_remote_copy(
            src_ref=src_ref, dst_ref=dst_ref, send_sem=send, recv_sem=recv,
            device_id={"wlk": dst}, device_id_type=MESH)

    def walker_copy(src, dst):
        return to_peer(pop.at[src], pop.at[src], p_send.at[dst], p_recv.at[src], dst)

    def tile_copy(src, dst):
        return to_peer(tile.at[src], tile.at[src], t_send.at[dst], t_recv.at[src], dst)

    def gradient_copy(src, dst):
        return to_peer(gsend.at[dst], grecv.at[src], g_send.at[dst], g_recv.at[src], dst)

    def energy_copy(src, dst):
        return to_peer(esend.at[dst], erecv.at[src], e_send.at[dst], e_recv.at[src], dst)

    loads = [
        pltpu.make_async_copy(src, dst, load_sem.at[i])
        for i, (src, dst) in enumerate((
            (orb_hbm, orb), (par_hbm, par), (logw_hbm, logw), (prop_hbm, prop)))
    ]
    for load in loads:
        load.start()
    load_orb, load_par, load_logw, load_prop = loads

    barrier = pltpu.get_barrier_semaphore()

    def greet_vec(j):
        pl.semaphore_signal(
            barrier, inc=1, device_id={"vec": by_distance(me, n_vec, j)}, device_id_type=MESH)

    def greet_wlk(j):
        pl.semaphore_signal(
            barrier, inc=1, device_id={"wlk": by_chip(mw, n_wlk, j)}, device_id_type=MESH)

    each(others, greet_vec)
    each(peers, greet_wlk)
    for slot in range(slots):
        in_slot(slot, lambda: own_copy(slot).start())
        if (slot + 1) * n_wlk > vecs:
            @pl.when(slot * n_wlk + place >= vecs)
            def _():
                shared[:, slot * occ:(slot + 1) * occ, :] = jnp.zeros(
                    (n_vec, occ, basis), jnp.bfloat16)
    load_orb.wait()
    pop[mw] = orb[...].astype(jnp.bfloat16)
    load_logw.wait()
    load_par.wait()
    tile[mw, 0:8] = jnp.broadcast_to(logw[...], (8, 128))
    tile[mw, 8:16] = jnp.broadcast_to(par[...], (8, 128)).astype(jnp.float32)
    pl.semaphore_wait(barrier, others + peers)

    for slot in range(slots):
        def send_vectors():
            def send_far():
                vector_copy(slot, me, far_end).start()

            if relayed:
                pl.when(near > 0)(send_far)
            else:
                send_far()
            each(others - 1, lambda j: vector_copy(
                slot, me, by_distance(me, n_vec, j + 1)).start())

        in_slot(slot, send_vectors)
    each(peers, lambda j: walker_copy(mw, by_chip(mw, n_wlk, j)).start())
    each(peers, lambda j: tile_copy(mw, by_chip(mw, n_wlk, j)).start())

    load_prop.wait()
    propb[...] = prop[...].astype(jnp.bfloat16)
    each(peers, lambda j: tile_copy(by_chip(mw, n_wlk, j), mw).wait_recv())
    each(peers, lambda j: walker_copy(by_chip(mw, n_wlk, j), mw).wait_recv())

    def pick(parent, read):
        value = read(0)
        for m in range(1, n_wlk):
            value = jnp.where(parent == m, read(m), value)
        return value

    for k in range(n_wlk):
        parent = jnp.broadcast_to(tile[k, 8:9, 0:1], (occ, basis))
        chosen[k] = pick(parent, lambda m: pop[m].astype(jnp.float32)).astype(jnp.bfloat16)
    chosen_log = pick(tile[mw, 8:16], lambda m: tile[m, 0:8])

    row = lax.broadcasted_iota(jnp.int32, (occ, occ), 0)
    col = lax.broadcasted_iota(jnp.int32, (occ, occ), 1)
    diagonal = row == col

    def contribution(source, finish):
        vectors = shared[source]
        for j in range(n_wlk):
            k = by_chip(mw, n_wlk, j) if j < peers else mw
            s = dot_t(vectors, chosen[k])
            blocks = []
            exchange = jnp.zeros((occ, occ), jnp.float32)
            squares = jnp.zeros((1, 1), jnp.float32)
            for g in range(slots):
                sg = s[g * occ:(g + 1) * occ, :]
                on_diagonal = jnp.where(diagonal, sg, 0.0)
                tg = jnp.sum(jnp.sum(on_diagonal, axis=0, keepdims=True), axis=1, keepdims=True)
                exchange = exchange + sg * sg.T
                squares = squares + tg * tg
                blocks.append((scale * (jnp.where(diagonal, tg, 0.0) - sg)).astype(jnp.bfloat16))
            adjoint = jnp.concatenate(blocks, axis=1) if slots > 1 else blocks[0]
            total = jnp.sum(jnp.sum(exchange, axis=0, keepdims=True), axis=1, keepdims=True)
            energy = jnp.broadcast_to(0.5 * scale * (squares - total), (8, 128))
            finish(j, k, dot(adjoint, vectors), energy)

    def begin(j, k, gradient, energy):
        acc[k] = gradient
        eacc[k] = energy

    def add(j, k, gradient, energy):
        acc[k] += gradient
        eacc[k] += energy

    def add_and_give(j, k, gradient, energy):
        if j == peers:
            add(j, k, gradient, energy)
            return
        gsend[k] = (acc[k] + gradient).astype(jnp.bfloat16)
        gradient_copy(mw, k).start()
        esend[k] = eacc[k] + energy
        energy_copy(mw, k).start()

    for slot in range(slots):
        in_slot(slot, lambda: own_copy(slot).wait())
    contribution(me, begin)

    def await_vectors(src):
        for slot in range(slots):
            in_slot(slot, lambda: vector_copy(slot, src, me).wait_recv())

    def serve(j):
        src = by_distance(me, n_vec, others - 1 - j)
        await_vectors(src)
        contribution(src, add)

    if relayed:
        serve(0)
        pl.when(near == 1)(relay)
        each(others - 2, lambda j: serve(j + 1))
        pl.when(near != 1)(lambda: await_vectors(far_end))
    else:
        each(others - 1, serve)
        await_vectors(far_end)
    contribution(far_end, add_and_give)

    acc[mw] = chosen[mw].astype(jnp.float32) - gradient_step * acc[mw]

    def collect(j):
        src = by_chip(mw, n_wlk, peers - 1 - j)
        gradient_copy(src, mw).wait_recv()
        acc[mw] -= gradient_step * grecv[src].astype(jnp.float32)

    def collect_energy(j):
        src = by_chip(mw, n_wlk, peers - 1 - j)
        energy_copy(src, mw).wait_recv()
        eacc[mw] += erecv[src]

    each(peers, collect)

    x = dot_t(acc[mw].astype(jnp.bfloat16), propb[...])
    mean_square = jnp.sum(jnp.sum(x * x, axis=0, keepdims=True), axis=1, keepdims=True)
    mean_square = mean_square / (occ * basis)
    x = x * (1.0 / jnp.sqrt(mean_square + epsilon))
    for _ in range(NS_ITERS):
        xb = x.astype(jnp.bfloat16)
        inter = (dot_t(xb, xb) / basis).astype(jnp.bfloat16)
        x = 0.5 * (3.0 * x - dot(inter, xb))
    out_ref[...] = x

    each(peers, collect_energy)
    outlog_ref[0] = jnp.max(chosen_log - energy_step * eacc[mw])

    def drain_vec(dst):
        for slot in range(slots):
            in_slot(slot, lambda: vector_copy(slot, me, dst).wait_send())

    def drain_relay():
        for slot in range(slots):
            in_slot(slot, lambda: relay_copy(slot).wait_send())

    def drain_wlk(j):
        dst = by_chip(mw, n_wlk, j)
        walker_copy(mw, dst).wait_send()
        tile_copy(mw, dst).wait_send()
        gradient_copy(mw, dst).wait_send()
        energy_copy(mw, dst).wait_send()

    if relayed:
        pl.when(near > 0)(lambda: drain_vec(far_end))
        pl.when(near == 1)(drain_relay)
    else:
        drain_vec(far_end)
    each(others - 1, lambda j: drain_vec(by_distance(me, n_vec, j + 1)))
    each(peers, drain_wlk)


def solution(mesh):
    n_vec, n_wlk = mesh.shape["vec"], mesh.shape["wlk"]

    def local(cholesky, orbitals, log_weights, parents, propagator):
        walkers, occ, basis = orbitals.shape
        assert walkers == 1
        vecs = cholesky.shape[0]
        slots = -(-vecs // n_wlk)
        f32, bf16 = jnp.float32, jnp.bfloat16
        dma = pltpu.SemaphoreType.DMA
        hbm = pl.BlockSpec(memory_space=pltpu.HBM)
        smem = pl.BlockSpec(memory_space=pltpu.SMEM)
        out, logs = pl.pallas_call(
            functools.partial(kernel, n_vec, n_wlk, vecs),
            out_shape=(
                jax.ShapeDtypeStruct((occ, basis), f32),
                jax.ShapeDtypeStruct((1,), f32),
            ),
            in_specs=[hbm] * 5,
            out_specs=(pl.BlockSpec(memory_space=pltpu.VMEM), smem),
            scratch_shapes=[
                pltpu.VMEM((1, 1), f32),
                pltpu.VMEM((1, 1), jnp.int32),
                pltpu.VMEM((occ, basis), f32),
                pltpu.VMEM(propagator.shape, f32),
                pltpu.VMEM(propagator.shape, bf16),
                pltpu.VMEM((n_wlk, occ, basis), bf16),
                pltpu.VMEM((n_wlk, 16, 128), f32),
                pltpu.VMEM((n_wlk, occ, basis), bf16),
                pltpu.VMEM((n_vec, slots * occ, basis), bf16),
                pltpu.VMEM((n_wlk, occ, basis), bf16),
                pltpu.VMEM((n_wlk, occ, basis), bf16),
                pltpu.VMEM((n_wlk, 8, 128), f32),
                pltpu.VMEM((n_wlk, 8, 128), f32),
                pltpu.VMEM((n_wlk, occ, basis), f32),
                pltpu.VMEM((n_wlk, 8, 128), f32),
                dma((4,)),
                dma((slots,)), dma((slots, n_vec)), dma((slots, n_vec)), dma((slots,)),
            ] + [dma((n_wlk,))] * 8,
            compiler_params=pltpu.CompilerParams(
                collective_id=0, has_side_effects=True, vmem_limit_bytes=67043328),
        )(
            cholesky.reshape(vecs * occ, basis),
            orbitals.reshape(occ, basis),
            log_weights.reshape(1, 1),
            parents.reshape(1, 1),
            propagator,
        )
        return out.reshape(orbitals.shape), logs

    placed = (
        P(("grp", "vec"), None, None),
        P(("grp", "vec", "wlk"), None, None),
        P(("grp", "vec", "wlk")),
        P(("grp", "vec", "wlk")),
        P("grp", None),
    )
    return jax.shard_map(
        local,
        mesh=mesh,
        in_specs=placed,
        out_specs=(P(("grp", "vec", "wlk"), None, None), P(("grp", "vec", "wlk"))),
        check_vma=False,
    )
```

```python
import functools
import math

import jax
import jax.numpy as jnp
from jax import lax
from jax.experimental import pallas as pl
from jax.experimental.pallas import tpu as pltpu
from jax.sharding import PartitionSpec as P

NS_ITERS = 2

gradient_step = 0.25
energy_step = 0.002
epsilon = 1e-06

MESH = pl.DeviceIdType.MESH
UNROLL_LIMIT = 8


def dot(a, b):
    return lax.dot_general(a, b, (((1,), (0,)), ((), ())), preferred_element_type=jnp.float32)


def dot_t(a, b):
    return lax.dot_general(a, b, (((1,), (1,)), ((), ())), preferred_element_type=jnp.float32)


def each(count, body):
    if count <= UNROLL_LIMIT:
        for j in range(count):
            body(j)
    else:
        lax.fori_loop(0, count, lambda j, c: (body(j), c)[1], 0)


def by_distance(me, n, j):
    side = lax.div(2 * me, n)
    near = me + side * (n - 1 - 2 * me)
    spot = n - 1 - j - lax.div(near + j + 1, n)
    return spot + side * (n - 1 - 2 * spot)


def by_chip(me, n, j):
    if n % 2:
        return lax.rem(me + 1 + j, n)
    step = j + 2
    core = lax.rem(me + lax.rem(step, 2) + lax.div(step, n), 2)
    return lax.rem((lax.div(me, 2) + lax.div(step, 2)) * 2 + core, n)


def kernel(
    n_vec, n_wlk, vecs,
    chol_hbm, orb_hbm, logw_hbm, par_hbm, prop_hbm,
    out_ref, outlog_ref,
    logw, par, orb, prop, propb, pop, tile, chosen, shared, gsend, grecv, esend, erecv, acc, eacc,
    load_sem, c_load, c_send, c_recv, r_send, p_send, p_recv, t_send, t_recv,
    g_send, g_recv, e_send, e_recv,
):
    me = lax.axis_index("vec")
    mw = lax.axis_index("wlk")
    occ, basis = orb.shape
    slots = shared.shape[1] // occ
    scale = 1.0 / math.sqrt(vecs * n_vec)
    others, peers = n_vec - 1, n_wlk - 1

    half = n_wlk // 2
    place = lax.rem(mw, 2) * half + lax.div(mw, 2) if n_wlk % 2 == 0 else mw

    def in_slot(slot, body):
        if (slot + 1) * n_wlk <= vecs:
            body()
        else:
            pl.when(slot * n_wlk + place < vecs)(body)

    def share(slot):
        return pl.ds(pl.multiple_of((slot * n_wlk + place) * occ, occ), occ)

    def spot(slot):
        return pl.ds(slot * occ, occ)

    def own_copy(slot):
        return pltpu.make_async_copy(
            chol_hbm.at[share(slot)], shared.at[me, spot(slot)], c_load.at[slot])

    def vector_copy(slot, src, dst):
        return pltpu.make_async_remote_copy(
            src_ref=chol_hbm.at[share(slot)], dst_ref=shared.at[src, spot(slot)],
            send_sem=c_send.at[slot, dst], recv_sem=c_recv.at[slot, src],
            device_id={"vec": dst}, device_id_type=MESH)

    side = lax.div(2 * me, n_vec)
    near = me + side * (n_vec - 1 - 2 * me)
    near_end, far_end = side * (n_vec - 1), n_vec - 1 - side * (n_vec - 1)
    relayed = n_vec >= 4

    def relay_copy(slot):
        return pltpu.make_async_remote_copy(
            src_ref=shared.at[far_end, spot(slot)], dst_ref=shared.at[far_end, spot(slot)],
            send_sem=r_send.at[slot], recv_sem=c_recv.at[slot, far_end],
            device_id={"vec": near_end}, device_id_type=MESH)

    def relay():
        for slot in range(slots):
            def forward():
                vector_copy(slot, far_end, me).wait_recv()
                relay_copy(slot).start()

            in_slot(slot, forward)

    def to_peer(src_ref, dst_ref, send, recv, dst):
        return pltpu.make_async_remote_copy(
            src_ref=src_ref, dst_ref=dst_ref, send_sem=send, recv_sem=recv,
            device_id={"wlk": dst}, device_id_type=MESH)

    def walker_copy(src, dst):
        return to_peer(pop.at[src], pop.at[src], p_send.at[dst], p_recv.at[src], dst)

    def tile_copy(src, dst):
        return to_peer(tile.at[src], tile.at[src], t_send.at[dst], t_recv.at[src], dst)

    def gradient_copy(src, dst):
        return to_peer(gsend.at[dst], grecv.at[src], g_send.at[dst], g_recv.at[src], dst)

    def energy_copy(src, dst):
        return to_peer(esend.at[dst], erecv.at[src], e_send.at[dst], e_recv.at[src], dst)

    loads = [
        pltpu.make_async_copy(src, dst, load_sem.at[i])
        for i, (src, dst) in enumerate((
            (orb_hbm, orb), (par_hbm, par), (logw_hbm, logw), (prop_hbm, prop)))
    ]
    for load in loads:
        load.start()
    load_orb, load_par, load_logw, load_prop = loads

    barrier = pltpu.get_barrier_semaphore()

    def greet_vec(j):
        pl.semaphore_signal(
            barrier, inc=1, device_id={"vec": by_distance(me, n_vec, j)}, device_id_type=MESH)

    def greet_wlk(j):
        pl.semaphore_signal(
            barrier, inc=1, device_id={"wlk": by_chip(mw, n_wlk, j)}, device_id_type=MESH)

    each(others, greet_vec)
    each(peers, greet_wlk)
    for slot in range(slots):
        in_slot(slot, lambda: own_copy(slot).start())
        if (slot + 1) * n_wlk > vecs:
            @pl.when(slot * n_wlk + place >= vecs)
            def _():
                shared[:, slot * occ:(slot + 1) * occ, :] = jnp.zeros(
                    (n_vec, occ, basis), jnp.bfloat16)
    pl.semaphore_wait(barrier, others + peers)

    for slot in range(slots):
        def send_vectors():
            def send_far():
                vector_copy(slot, me, far_end).start()

            if relayed:
                pl.when(near > 0)(send_far)
            else:
                send_far()
            each(others - 1, lambda j: vector_copy(
                slot, me, by_distance(me, n_vec, j + 1)).start())

        in_slot(slot, send_vectors)
    load_orb.wait()
    pop[mw] = orb[...].astype(jnp.bfloat16)
    load_logw.wait()
    load_par.wait()
    tile[mw, 0:8] = jnp.broadcast_to(logw[...], (8, 128))
    tile[mw, 8:16] = jnp.broadcast_to(par[...], (8, 128)).astype(jnp.float32)
    each(peers, lambda j: walker_copy(mw, by_chip(mw, n_wlk, j)).start())
    each(peers, lambda j: tile_copy(mw, by_chip(mw, n_wlk, j)).start())

    load_prop.wait()
    propb[...] = prop[...].T.astype(jnp.bfloat16)
    each(peers, lambda j: tile_copy(by_chip(mw, n_wlk, j), mw).wait_recv())
    each(peers, lambda j: walker_copy(by_chip(mw, n_wlk, j), mw).wait_recv())

    def pick(parent, read):
        value = read(0)
        for m in range(1, n_wlk):
            value = jnp.where(parent == m, read(m), value)
        return value

    for k in range(n_wlk):
        parent = jnp.broadcast_to(tile[k, 8:9, 0:1], (occ, basis))
        chosen[k] = pick(parent, lambda m: pop[m].astype(jnp.float32)).astype(jnp.bfloat16)
    chosen_log = pick(tile[mw, 8:16], lambda m: tile[m, 0:8])

    row = lax.broadcasted_iota(jnp.int32, (occ, occ), 0)
    col = lax.broadcasted_iota(jnp.int32, (occ, occ), 1)
    diagonal = row == col

    def contribution(source, finish):
        vectors = shared[source]
        order = [by_chip(mw, n_wlk, j) for j in range(peers)] + [mw]
        products = [dot_t(vectors, chosen[k]) for k in order]
        parts = []
        for s in products:
            blocks = []
            exchange = jnp.zeros((occ, occ), jnp.float32)
            squares = jnp.zeros((1, 1), jnp.float32)
            for g in range(slots):
                sg = s[g * occ:(g + 1) * occ, :]
                on_diagonal = jnp.where(diagonal, sg, 0.0)
                tg = jnp.sum(jnp.sum(on_diagonal, axis=0, keepdims=True), axis=1, keepdims=True)
                exchange = exchange + sg * sg.T
                squares = squares + tg * tg
                blocks.append((scale * (jnp.where(diagonal, tg, 0.0) - sg)).astype(jnp.bfloat16))
            adjoint = jnp.concatenate(blocks, axis=1) if slots > 1 else blocks[0]
            total = jnp.sum(jnp.sum(exchange, axis=0, keepdims=True), axis=1, keepdims=True)
            energy = jnp.broadcast_to(0.5 * scale * (squares - total), (8, 128))
            parts.append((dot(adjoint, vectors), energy))
        for j, (gradient, energy) in enumerate(parts):
            finish(j, order[j], gradient, energy)

    def begin(j, k, gradient, energy):
        acc[k] = gradient
        eacc[k] = energy

    def add(j, k, gradient, energy):
        acc[k] += gradient
        eacc[k] += energy

    def add_and_give(j, k, gradient, energy):
        if j == peers:
            add(j, k, gradient, energy)
            return
        gsend[k] = (acc[k] + gradient).astype(jnp.bfloat16)
        gradient_copy(mw, k).start()
        esend[k] = eacc[k] + energy
        energy_copy(mw, k).start()

    for slot in range(slots):
        in_slot(slot, lambda: own_copy(slot).wait())
    contribution(me, begin)

    def await_vectors(src):
        for slot in range(slots):
            in_slot(slot, lambda: vector_copy(slot, src, me).wait_recv())

    def serve(j):
        src = by_distance(me, n_vec, others - 1 - j)
        await_vectors(src)
        contribution(src, add)

    if relayed:
        serve(0)
        pl.when(near == 1)(relay)
        each(others - 2, lambda j: serve(j + 1))
        pl.when(near != 1)(lambda: await_vectors(far_end))
    else:
        each(others - 1, serve)
        await_vectors(far_end)
    contribution(far_end, add_and_give)

    acc[mw] = chosen[mw].astype(jnp.float32) - gradient_step * acc[mw]

    def collect(j):
        src = by_chip(mw, n_wlk, peers - 1 - j)
        gradient_copy(src, mw).wait_recv()
        acc[mw] -= gradient_step * grecv[src].astype(jnp.float32)

    def collect_energy(j):
        src = by_chip(mw, n_wlk, peers - 1 - j)
        energy_copy(src, mw).wait_recv()
        eacc[mw] += erecv[src]

    each(peers, collect)

    x = dot(acc[mw].astype(jnp.bfloat16), propb[...])
    mean_square = jnp.sum(jnp.sum(x * x, axis=0, keepdims=True), axis=1, keepdims=True)
    mean_square = mean_square / (occ * basis)
    norm = 1.0 / jnp.sqrt(mean_square + epsilon)
    for step in range(NS_ITERS):
        xb = x.astype(jnp.bfloat16)
        inter = dot_t(xb, xb) * (norm * norm / basis if step == 0 else 1.0 / basis)
        x = 0.5 * (3.0 * x - dot(inter.astype(jnp.bfloat16), xb))
        if step == 0:
            x = norm * x
    out_ref[...] = x

    each(peers, collect_energy)
    outlog_ref[0] = jnp.max(chosen_log - energy_step * eacc[mw])

    def drain_vec(dst):
        for slot in range(slots):
            in_slot(slot, lambda: vector_copy(slot, me, dst).wait_send())

    def drain_relay():
        for slot in range(slots):
            in_slot(slot, lambda: relay_copy(slot).wait_send())

    def drain_wlk(j):
        dst = by_chip(mw, n_wlk, j)
        walker_copy(mw, dst).wait_send()
        tile_copy(mw, dst).wait_send()
        gradient_copy(mw, dst).wait_send()
        energy_copy(mw, dst).wait_send()

    if relayed:
        pl.when(near > 0)(lambda: drain_vec(far_end))
        pl.when(near == 1)(drain_relay)
    else:
        drain_vec(far_end)
    each(others - 1, lambda j: drain_vec(by_distance(me, n_vec, j + 1)))
    each(peers, drain_wlk)


def solution(mesh):
    n_vec, n_wlk = mesh.shape["vec"], mesh.shape["wlk"]

    def local(cholesky, orbitals, log_weights, parents, propagator):
        walkers, occ, basis = orbitals.shape
        assert walkers == 1
        vecs = cholesky.shape[0]
        slots = -(-vecs // n_wlk)
        f32, bf16 = jnp.float32, jnp.bfloat16
        dma = pltpu.SemaphoreType.DMA
        hbm = pl.BlockSpec(memory_space=pltpu.HBM)
        smem = pl.BlockSpec(memory_space=pltpu.SMEM)
        out, logs = pl.pallas_call(
            functools.partial(kernel, n_vec, n_wlk, vecs),
            out_shape=(
                pltpu.VMEM((occ, basis), f32),
                jax.ShapeDtypeStruct((1,), f32),
            ),
            in_specs=[hbm] * 5,
            out_specs=(pl.BlockSpec(memory_space=pltpu.VMEM), smem),
            scratch_shapes=[
                pltpu.VMEM((1, 1), f32),
                pltpu.VMEM((1, 1), jnp.int32),
                pltpu.VMEM((occ, basis), f32),
                pltpu.VMEM(propagator.shape, f32),
                pltpu.VMEM(propagator.shape, bf16),
                pltpu.VMEM((n_wlk, occ, basis), bf16),
                pltpu.VMEM((n_wlk, 16, 128), f32),
                pltpu.VMEM((n_wlk, occ, basis), bf16),
                pltpu.VMEM((n_vec, slots * occ, basis), bf16),
                pltpu.VMEM((n_wlk, occ, basis), bf16),
                pltpu.VMEM((n_wlk, occ, basis), bf16),
                pltpu.VMEM((n_wlk, 8, 128), f32),
                pltpu.VMEM((n_wlk, 8, 128), f32),
                pltpu.VMEM((n_wlk, occ, basis), f32),
                pltpu.VMEM((n_wlk, 8, 128), f32),
                dma((4,)),
                dma((slots,)), dma((slots, n_vec)), dma((slots, n_vec)), dma((slots,)),
            ] + [dma((n_wlk,))] * 8,
            compiler_params=pltpu.CompilerParams(
                collective_id=0, has_side_effects=True, vmem_limit_bytes=66400000),
        )(
            cholesky.reshape(vecs * occ, basis),
            orbitals.reshape(occ, basis),
            log_weights.reshape(1, 1),
            parents.reshape(1, 1),
            propagator,
        )
        return out.reshape(orbitals.shape), logs

    placed = (
        P(("grp", "vec"), None, None),
        P(("grp", "vec", "wlk"), None, None),
        P(("grp", "vec", "wlk")),
        P(("grp", "vec", "wlk")),
        P("grp", None),
    )
    return jax.shard_map(
        local,
        mesh=mesh,
        in_specs=placed,
        out_specs=(P(("grp", "vec", "wlk"), None, None), P(("grp", "vec", "wlk"))),
        check_vma=False,
    )
```

```python
import functools
import math

import jax
import jax.numpy as jnp
from jax import lax
from jax.experimental import pallas as pl
from jax.experimental.pallas import tpu as pltpu
from jax.sharding import PartitionSpec as P

NS_ITERS = 2

gradient_step = 0.25
energy_step = 0.002
epsilon = 1e-06

MESH = pl.DeviceIdType.MESH
UNROLL_LIMIT = 8


def dot(a, b):
    return lax.dot_general(a, b, (((1,), (0,)), ((), ())), preferred_element_type=jnp.float32)


def dot_t(a, b):
    return lax.dot_general(a, b, (((1,), (1,)), ((), ())), preferred_element_type=jnp.float32)


def each(count, body):
    if count <= UNROLL_LIMIT:
        for j in range(count):
            body(j)
    else:
        lax.fori_loop(0, count, lambda j, c: (body(j), c)[1], 0)


def by_distance(me, n, j):
    side = lax.div(2 * me, n)
    near = me + side * (n - 1 - 2 * me)
    spot = n - 1 - j - lax.div(near + j + 1, n)
    return spot + side * (n - 1 - 2 * spot)


def by_chip(me, n, j):
    if n % 2:
        return lax.rem(me + 1 + j, n)
    step = j + 2
    core = lax.rem(me + lax.rem(step, 2) + lax.div(step, n), 2)
    return lax.rem((lax.div(me, 2) + lax.div(step, 2)) * 2 + core, n)


def kernel(
    n_vec, n_wlk, vecs,
    chol_hbm, orb_hbm, logw_hbm, par_hbm, prop_hbm,
    out_ref, outlog_ref,
    logw, par, orb, prop, propb, pop, tile, chosen, turned, shared, gsend, grecv, esend, erecv, acc, eacc,
    load_sem, c_load, c_send, c_recv, r_send, p_send, p_recv, t_send, t_recv,
    g_send, g_recv, e_send, e_recv,
):
    me = lax.axis_index("vec")
    mw = lax.axis_index("wlk")
    occ, basis = orb.shape
    slots = shared.shape[1] // occ
    scale = 1.0 / math.sqrt(vecs * n_vec)
    others, peers = n_vec - 1, n_wlk - 1

    half = n_wlk // 2
    place = lax.rem(mw, 2) * half + lax.div(mw, 2) if n_wlk % 2 == 0 else mw

    def in_slot(slot, body):
        if (slot + 1) * n_wlk <= vecs:
            body()
        else:
            pl.when(slot * n_wlk + place < vecs)(body)

    def share(slot):
        return pl.ds(pl.multiple_of((slot * n_wlk + place) * occ, occ), occ)

    def spot(slot):
        return pl.ds(slot * occ, occ)

    def own_copy(slot):
        return pltpu.make_async_copy(
            chol_hbm.at[share(slot)], shared.at[me, spot(slot)], c_load.at[slot])

    def vector_copy(slot, src, dst):
        return pltpu.make_async_remote_copy(
            src_ref=chol_hbm.at[share(slot)], dst_ref=shared.at[src, spot(slot)],
            send_sem=c_send.at[slot, dst], recv_sem=c_recv.at[slot, src],
            device_id={"vec": dst}, device_id_type=MESH)

    side = lax.div(2 * me, n_vec)
    near = me + side * (n_vec - 1 - 2 * me)
    near_end, far_end = side * (n_vec - 1), n_vec - 1 - side * (n_vec - 1)
    relayed = n_vec >= 4

    def relay_copy(slot):
        return pltpu.make_async_remote_copy(
            src_ref=shared.at[far_end, spot(slot)], dst_ref=shared.at[far_end, spot(slot)],
            send_sem=r_send.at[slot], recv_sem=c_recv.at[slot, far_end],
            device_id={"vec": near_end}, device_id_type=MESH)

    def relay():
        for slot in range(slots):
            def forward():
                vector_copy(slot, far_end, me).wait_recv()
                relay_copy(slot).start()

            in_slot(slot, forward)

    def to_peer(src_ref, dst_ref, send, recv, dst):
        return pltpu.make_async_remote_copy(
            src_ref=src_ref, dst_ref=dst_ref, send_sem=send, recv_sem=recv,
            device_id={"wlk": dst}, device_id_type=MESH)

    def walker_copy(src, dst):
        return to_peer(pop.at[src], pop.at[src], p_send.at[dst], p_recv.at[src], dst)

    def tile_copy(src, dst):
        return to_peer(tile.at[src], tile.at[src], t_send.at[dst], t_recv.at[src], dst)

    def gradient_copy(src, dst):
        return to_peer(gsend.at[dst], grecv.at[src], g_send.at[dst], g_recv.at[src], dst)

    def energy_copy(src, dst):
        return to_peer(esend.at[dst], erecv.at[src], e_send.at[dst], e_recv.at[src], dst)

    loads = [
        pltpu.make_async_copy(src, dst, load_sem.at[i])
        for i, (src, dst) in enumerate((
            (orb_hbm, orb), (par_hbm, par), (logw_hbm, logw), (prop_hbm, prop)))
    ]
    for load in loads:
        load.start()
    load_orb, load_par, load_logw, load_prop = loads

    barrier = pltpu.get_barrier_semaphore()

    def greet_vec(j):
        pl.semaphore_signal(
            barrier, inc=1, device_id={"vec": by_distance(me, n_vec, j)}, device_id_type=MESH)

    def greet_wlk(j):
        pl.semaphore_signal(
            barrier, inc=1, device_id={"wlk": by_chip(mw, n_wlk, j)}, device_id_type=MESH)

    each(others, greet_vec)
    each(peers, greet_wlk)
    for slot in range(slots):
        in_slot(slot, lambda: own_copy(slot).start())
        if (slot + 1) * n_wlk > vecs:
            @pl.when(slot * n_wlk + place >= vecs)
            def _():
                shared[:, slot * occ:(slot + 1) * occ, :] = jnp.zeros(
                    (n_vec, occ, basis), jnp.bfloat16)
    pl.semaphore_wait(barrier, others + peers)

    for slot in range(slots):
        def send_vectors():
            def send_far():
                vector_copy(slot, me, far_end).start()

            if relayed:
                pl.when(near > 0)(send_far)
            else:
                send_far()
            each(others - 1, lambda j: vector_copy(
                slot, me, by_distance(me, n_vec, j + 1)).start())

        in_slot(slot, send_vectors)
    load_orb.wait()
    pop[mw] = orb[...].astype(jnp.bfloat16)
    load_logw.wait()
    load_par.wait()
    tile[mw, 0:8] = jnp.broadcast_to(logw[...], (8, 128))
    tile[mw, 8:16] = jnp.broadcast_to(par[...], (8, 128)).astype(jnp.float32)
    each(peers, lambda j: walker_copy(mw, by_chip(mw, n_wlk, j)).start())
    each(peers, lambda j: tile_copy(mw, by_chip(mw, n_wlk, j)).start())

    load_prop.wait()
    propb[...] = prop[...].T.astype(jnp.bfloat16)
    each(peers, lambda j: tile_copy(by_chip(mw, n_wlk, j), mw).wait_recv())
    each(peers, lambda j: walker_copy(by_chip(mw, n_wlk, j), mw).wait_recv())

    def pick(parent, read):
        value = read(0)
        for m in range(1, n_wlk):
            value = jnp.where(parent == m, read(m), value)
        return value

    for k in range(n_wlk):
        parent = jnp.broadcast_to(tile[k, 8:9, 0:1], (occ, basis))
        rows = pick(parent, lambda m: pop[m].astype(jnp.float32))
        chosen[k] = rows.astype(jnp.bfloat16)
        turned[k] = rows.T.astype(jnp.bfloat16)
    chosen_log = pick(tile[mw, 8:16], lambda m: tile[m, 0:8])

    row = lax.broadcasted_iota(jnp.int32, (occ, occ), 0)
    col = lax.broadcasted_iota(jnp.int32, (occ, occ), 1)
    diagonal = row == col

    def contribution(source, finish):
        vectors = shared[source]
        order = [by_chip(mw, n_wlk, j) for j in range(peers)] + [mw]
        products = [dot(vectors, turned[k]) for k in order]
        parts = []
        for s in products:
            blocks = []
            exchange = jnp.zeros((occ, occ), jnp.float32)
            squares = jnp.zeros((1, 1), jnp.float32)
            for g in range(slots):
                sg = s[g * occ:(g + 1) * occ, :]
                on_diagonal = jnp.where(diagonal, sg, 0.0)
                tg = jnp.sum(jnp.sum(on_diagonal, axis=0, keepdims=True), axis=1, keepdims=True)
                exchange = exchange + sg * sg.T
                squares = squares + tg * tg
                blocks.append((scale * (jnp.where(diagonal, tg, 0.0) - sg)).astype(jnp.bfloat16))
            adjoint = jnp.concatenate(blocks, axis=1) if slots > 1 else blocks[0]
            total = jnp.sum(jnp.sum(exchange, axis=0, keepdims=True), axis=1, keepdims=True)
            energy = jnp.broadcast_to(0.5 * scale * (squares - total), (8, 128))
            parts.append((dot(adjoint, vectors), energy))
        for j, (gradient, energy) in enumerate(parts):
            finish(j, order[j], gradient, energy)

    def begin(j, k, gradient, energy):
        acc[k] = gradient
        eacc[k] = energy

    def add(j, k, gradient, energy):
        acc[k] += gradient
        eacc[k] += energy

    def add_and_give(j, k, gradient, energy):
        if j == peers:
            add(j, k, gradient, energy)
            return
        esend[k] = eacc[k] + energy
        energy_copy(mw, k).start()
        gsend[k] = (acc[k] + gradient).astype(jnp.bfloat16)
        gradient_copy(mw, k).start()

    for slot in range(slots):
        in_slot(slot, lambda: own_copy(slot).wait())
    contribution(me, begin)

    def await_vectors(src):
        for slot in range(slots):
            in_slot(slot, lambda: vector_copy(slot, src, me).wait_recv())

    def serve(j):
        src = by_distance(me, n_vec, others - 1 - j)
        await_vectors(src)
        contribution(src, add)

    if relayed:
        serve(0)
        pl.when(near == 1)(relay)
        each(others - 2, lambda j: serve(j + 1))
        pl.when(near != 1)(lambda: await_vectors(far_end))
    else:
        each(others - 1, serve)
        await_vectors(far_end)
    contribution(far_end, add_and_give)

    acc[mw] = chosen[mw].astype(jnp.float32) - gradient_step * acc[mw]

    def collect(j):
        src = by_chip(mw, n_wlk, peers - 1 - j)
        gradient_copy(src, mw).wait_recv()
        acc[mw] -= gradient_step * grecv[src].astype(jnp.float32)

    def collect_energy(j):
        src = by_chip(mw, n_wlk, peers - 1 - j)
        energy_copy(src, mw).wait_recv()
        eacc[mw] += erecv[src]

    each(peers, collect)
    each(peers, collect_energy)
    outlog_ref[0] = jnp.max(chosen_log - energy_step * eacc[mw])

    x = dot(acc[mw].astype(jnp.bfloat16), propb[...])
    mean_square = jnp.sum(jnp.sum(x * x, axis=0, keepdims=True), axis=1, keepdims=True)
    mean_square = mean_square / (occ * basis)
    norm = 1.0 / jnp.sqrt(mean_square + epsilon)
    for step in range(NS_ITERS):
        xb = x.astype(jnp.bfloat16)
        inter = dot_t(xb, xb) * (norm * norm / basis if step == 0 else 1.0 / basis)
        x = 0.5 * (3.0 * x - dot(inter.astype(jnp.bfloat16), xb))
        if step == 0:
            x = norm * x
    out_ref[...] = x


    def drain_vec(dst):
        for slot in range(slots):
            in_slot(slot, lambda: vector_copy(slot, me, dst).wait_send())

    def drain_relay():
        for slot in range(slots):
            in_slot(slot, lambda: relay_copy(slot).wait_send())

    def drain_wlk(j):
        dst = by_chip(mw, n_wlk, j)
        walker_copy(mw, dst).wait_send()
        tile_copy(mw, dst).wait_send()
        gradient_copy(mw, dst).wait_send()
        energy_copy(mw, dst).wait_send()

    if relayed:
        pl.when(near > 0)(lambda: drain_vec(far_end))
        pl.when(near == 1)(drain_relay)
    else:
        drain_vec(far_end)
    each(others - 1, lambda j: drain_vec(by_distance(me, n_vec, j + 1)))
    each(peers, drain_wlk)


def solution(mesh):
    n_vec, n_wlk = mesh.shape["vec"], mesh.shape["wlk"]

    def local(cholesky, orbitals, log_weights, parents, propagator):
        walkers, occ, basis = orbitals.shape
        assert walkers == 1
        vecs = cholesky.shape[0]
        slots = -(-vecs // n_wlk)
        f32, bf16 = jnp.float32, jnp.bfloat16
        dma = pltpu.SemaphoreType.DMA
        hbm = pl.BlockSpec(memory_space=pltpu.HBM)
        smem = pl.BlockSpec(memory_space=pltpu.SMEM)
        out, logs = pl.pallas_call(
            functools.partial(kernel, n_vec, n_wlk, vecs),
            out_shape=(
                pltpu.VMEM((occ, basis), f32),
                jax.ShapeDtypeStruct((1,), f32),
            ),
            in_specs=[hbm] * 5,
            out_specs=(pl.BlockSpec(memory_space=pltpu.VMEM), smem),
            scratch_shapes=[
                pltpu.VMEM((1, 1), f32),
                pltpu.VMEM((1, 1), jnp.int32),
                pltpu.VMEM((occ, basis), f32),
                pltpu.VMEM(propagator.shape, f32),
                pltpu.VMEM(propagator.shape, bf16),
                pltpu.VMEM((n_wlk, occ, basis), bf16),
                pltpu.VMEM((n_wlk, 16, 128), f32),
                pltpu.VMEM((n_wlk, occ, basis), bf16),
                pltpu.VMEM((n_wlk, basis, occ), bf16),
                pltpu.VMEM((n_vec, slots * occ, basis), bf16),
                pltpu.VMEM((n_wlk, occ, basis), bf16),
                pltpu.VMEM((n_wlk, occ, basis), bf16),
                pltpu.VMEM((n_wlk, 8, 128), f32),
                pltpu.VMEM((n_wlk, 8, 128), f32),
                pltpu.VMEM((n_wlk, occ, basis), f32),
                pltpu.VMEM((n_wlk, 8, 128), f32),
                dma((4,)),
                dma((slots,)), dma((slots, n_vec)), dma((slots, n_vec)), dma((slots,)),
            ] + [dma((n_wlk,))] * 8,
            compiler_params=pltpu.CompilerParams(
                collective_id=0, has_side_effects=True, vmem_limit_bytes=66400000),
        )(
            cholesky.reshape(vecs * occ, basis),
            orbitals.reshape(occ, basis),
            log_weights.reshape(1, 1),
            parents.reshape(1, 1),
            propagator,
        )
        return out.reshape(orbitals.shape), logs

    placed = (
        P(("grp", "vec"), None, None),
        P(("grp", "vec", "wlk"), None, None),
        P(("grp", "vec", "wlk")),
        P(("grp", "vec", "wlk")),
        P("grp", None),
    )
    return jax.shard_map(
        local,
        mesh=mesh,
        in_specs=placed,
        out_specs=(P(("grp", "vec", "wlk"), None, None), P(("grp", "vec", "wlk"))),
        check_vma=False,
    )
```
